256 devices in a mesh: snap: 16 (over z, x_hi), mesh: 16 (over x_lo, y, core).
Axes of the slice: x: 4 (x_hi: 2, x_lo: 2; x = x_hi * 2 + x_lo), y: 4, z: 8, core: 2. Of those that a mesh axis runs over, the one named last changes fastest.
Arguments:
- snapshots: float32 [49152, 2048], P('mesh', 'snap'), may hold values from -6 to 6
- region_ids: int32 [96, 512], P('mesh'), may hold values from 0 to 7
- conductivity: float32 [8], replicated, may hold values from 0.2 to 5
Outputs:
- gram: float32 [2048, 2048], P('snap', 'mesh')
The draws below stay inside these ranges and needn't reach their ends.
All inputs are finite; a program needn't handle non-finite values.
Results may differ from the reference program's by a relative error of at most 0.0003.
Values sent between devices are 32-bit elements; how exact they have to be, the bound alone decides.
A program may use at most 128 MiB of HBM per device.

```python
import math
import jax
import jax.numpy as jnp
from jax import lax

RY = 512
SNAP_DEV = 128
REGIONS = 8
NX = 96
NODES = 49152
SNAPS = 2048


def set_ends(entries, stream_key, low, top_value):
    longest = entries.shape.index(max(entries.shape))
    spots = []
    for shift in (0, 1):
        where = [jax.random.randint(jax.random.fold_in(stream_key, axis), (), 0, length) for axis, length in enumerate(entries.shape)]
        where[longest] = (where[longest] + shift) % entries.shape[longest]
        spots.append(tuple(where))
    return entries.at[spots[0]].set(low).at[spots[1]].set(top_value)


def block_scale(stream_key, dims, cuts, smallest, largest):
    def one(position, parts):
        steps = jax.random.uniform(jax.random.fold_in(jax.random.fold_in(stream_key, 6), position), (parts,), jnp.float32, smallest / len(cuts), largest / len(cuts))
        return jnp.repeat(jnp.exp(steps), dims[position] // parts).reshape((-1,) + (1,) * (len(dims) - position - 1))

    gain = one(*cuts[0])
    for cut in cuts[1:]:
        gain = gain * one(*cut)
    return gain


def normal_values(rng, dims, spread, reach, cuts=(), kind=jnp.bfloat16):
    factor_of = block_scale(rng, dims, cuts, -0.22, 0.18) if cuts else 1.0
    values = jax.random.normal(rng, dims, jnp.float32) * spread * factor_of
    return jnp.minimum(jnp.maximum(values, -reach), reach).astype(kind)


def setup_inputs(seed: int = 0) -> dict:
    key_of = jax.random.split(jax.random.key(seed), 4)
    snapshots = normal_values(key_of[0], (NODES, SNAPS), 1.0, 6.0, ((0, 16), (1, 16)), jnp.float32)
    region_ids = set_ends(jax.random.randint(key_of[1], (NX, RY), 0, REGIONS), jax.random.fold_in(key_of[1], 1), 0, REGIONS - 1).astype(jnp.int32)
    conductivity = jnp.clip(jnp.exp(jax.random.uniform(key_of[2], (REGIONS,), jnp.float32, math.log(0.2), math.log(5.0))), 0.2, 5.0)
    return {"snapshots": snapshots, "region_ids": region_ids, "conductivity": conductivity}


def weights_of(region_ids, conductivity):
    table = jnp.arange(conductivity.shape[0], dtype=jnp.int32)
    picked = jnp.where(region_ids[:, :, None] == table[None, None, :], conductivity[None, None, :], jnp.zeros((), conductivity.dtype))
    return lax.optimization_barrier(jnp.sum(picked, axis=-1)) / 36.0

def element_terms(field, below, weight):
    lower = jnp.concatenate([field, below[None]], 0)
    padded = jnp.pad(lower, ((0, 0), (0, 1), (0, 0)))
    corner_a = padded[:-1, :-1]
    corner_b = padded[:-1, 1:]
    corner_e = padded[1:, :-1]
    corner_d = padded[1:, 1:]
    scaled = weight[:, :, None]
    to_a = scaled * (4.0 * corner_a + 2.0 * corner_b + 2.0 * corner_e + corner_d)
    to_b = scaled * (2.0 * corner_a + 4.0 * corner_b + corner_e + 2.0 * corner_d)
    to_e = scaled * (2.0 * corner_a + corner_b + 4.0 * corner_e + 2.0 * corner_d)
    to_d = scaled * (corner_a + 2.0 * corner_b + 2.0 * corner_e + 4.0 * corner_d)
    total = jnp.pad(to_a, ((0, 1), (0, 1), (0, 0))) + jnp.pad(to_b, ((0, 1), (1, 0), (0, 0)))
    total = total + jnp.pad(to_e, ((1, 0), (0, 1), (0, 0))) + jnp.pad(to_d, ((1, 0), (1, 0), (0, 0)))
    return total

def reference(snapshots, region_ids, conductivity):
    weight = weights_of(region_ids, conductivity)
    blocks = SNAPS // SNAP_DEV

    def one_block(index):
        start = (index * SNAP_DEV).astype(jnp.int32)
        columns = lax.dynamic_slice_in_dim(snapshots, start, SNAP_DEV, 1)
        field = columns.reshape(NX, RY, SNAP_DEV)
        below = jnp.zeros((RY, SNAP_DEV), snapshots.dtype)
        total = element_terms(field, below, weight)
        return total[:NX, :RY].reshape(NODES, SNAP_DEV)
    stacked = lax.map(one_block, jnp.arange(blocks, dtype=jnp.int32))
    panel = jnp.transpose(stacked, (1, 0, 2)).reshape(NODES, SNAPS)
    gram = jnp.dot(snapshots.T, panel, precision=lax.Precision.HIGHEST, preferred_element_type=jnp.float32)
    return gram / math.sqrt(NODES)
```

```python
import math

import jax
import jax.numpy as jnp
from jax import lax
from jax.sharding import Mesh
from jax.sharding import PartitionSpec as P


def passed_along(value, axis, steps):
    count = lax.axis_size(axis)
    first, last = (max(0, -steps), min(count, count - steps))
    return lax.ppermute(value, axis, [(source, source + steps) for source in range(first, last)])


def weights_of(region_ids, conductivity):
    table = jnp.arange(conductivity.shape[0], dtype=jnp.int32)
    picked = jnp.where(
        region_ids[:, :, None] == table[None, None, :],
        conductivity[None, None, :],
        jnp.zeros((), conductivity.dtype),
    )
    return jnp.sum(picked, axis=-1) / 36.0


def element_terms(field, below, weight):
    lower = jnp.concatenate([field, below[None]], 0)
    padded = jnp.pad(lower, ((0, 0), (0, 1), (0, 0)))
    corner_a = padded[:-1, :-1]
    corner_b = padded[:-1, 1:]
    corner_e = padded[1:, :-1]
    corner_d = padded[1:, 1:]
    scaled = weight[:, :, None]
    to_a = scaled * (4.0 * corner_a + 2.0 * corner_b + 2.0 * corner_e + corner_d)
    to_b = scaled * (2.0 * corner_a + 4.0 * corner_b + corner_e + 2.0 * corner_d)
    to_e = scaled * (2.0 * corner_a + corner_b + 4.0 * corner_e + 2.0 * corner_d)
    to_d = scaled * (corner_a + 2.0 * corner_b + 2.0 * corner_e + 4.0 * corner_d)
    total = jnp.pad(to_a, ((0, 1), (0, 1), (0, 0))) + jnp.pad(to_b, ((0, 1), (1, 0), (0, 0)))
    total = (
        total + jnp.pad(to_e, ((1, 0), (0, 1), (0, 0))) + jnp.pad(to_d, ((1, 0), (1, 0), (0, 0)))
    )
    return total


def contract(left, right):
    return lax.dot_general(
        left,
        right,
        (((0,), (0,)), ((), ())),
        precision=lax.Precision.HIGHEST,
        preferred_element_type=jnp.float32,
    )


def local(snapshots, region_ids, conductivity):
    strip, width = region_ids.shape
    node_rows, group_cols = snapshots.shape
    side = lax.axis_size("c")
    tiles = lax.axis_size("mesh")
    field = snapshots.reshape(strip, width, group_cols)
    weight = weights_of(region_ids, conductivity)
    below = passed_along(field[0], "mesh", -1)
    total = element_terms(field, below, weight)
    carried = passed_along(total[strip, :width], "mesh", 1)
    inner = total[:strip, :width]
    panel = jnp.concatenate([inner[:1] + carried[None], inner[1:]], 0).reshape(
        node_rows, group_cols
    )
    rows = lax.all_gather(snapshots, "c", axis=1, tiled=True)
    cols = lax.all_gather(panel, "r", axis=1, tiled=True)
    partial_value = contract(rows, cols)
    pieces = (
        partial_value.reshape(side, group_cols, side, group_cols)
        .transpose(0, 2, 1, 3)
        .reshape(side * side, group_cols, group_cols)
    )
    summed = lax.psum_scatter(pieces, "mesh", scatter_dimension=0, tiled=True)[0]
    perm = []
    for c in range(side):
        for t in range(tiles):
            dest_c, dest_t = t // side, c + side * (t % side)
            perm.append((c * tiles + t, dest_c * tiles + dest_t))
    placed = lax.ppermute(summed, ("c", "mesh"), perm)
    total_nodes = node_rows * tiles
    return placed / math.sqrt(total_nodes)


def solution(mesh):
    snap = mesh.shape["snap"]
    side = math.isqrt(snap)
    grid = Mesh(
        mesh.devices.reshape(snap // side, side, mesh.shape["mesh"]), ("r", "c", "mesh")
    )
    return jax.shard_map(
        local,
        mesh=grid,
        in_specs=(P("mesh", ("r", "c")), P("mesh", None), P()),
        out_specs=P(("r", "c"), "mesh"),
        check_vma=False,
    )
```

```python
import math

import jax
import jax.numpy as jnp
from jax import lax
from jax.sharding import Mesh
from jax.sharding import PartitionSpec as P


def passed_along(value, axis, steps):
    count = lax.axis_size(axis)
    first, last = (max(0, -steps), min(count, count - steps))
    return lax.ppermute(value, axis, [(source, source + steps) for source in range(first, last)])


def weights_of(region_ids, conductivity):
    table = jnp.arange(conductivity.shape[0], dtype=jnp.int32)
    picked = jnp.where(
        region_ids[:, :, None] == table[None, None, :],
        conductivity[None, None, :],
        jnp.zeros((), conductivity.dtype),
    )
    return jnp.sum(picked, axis=-1) / 36.0


def element_terms(field, below, weight):
    lower = jnp.concatenate([field, below[None]], 0)
    padded = jnp.pad(lower, ((0, 0), (0, 1), (0, 0)))
    corner_a = padded[:-1, :-1]
    corner_b = padded[:-1, 1:]
    corner_e = padded[1:, :-1]
    corner_d = padded[1:, 1:]
    scaled = weight[:, :, None]
    to_a = scaled * (4.0 * corner_a + 2.0 * corner_b + 2.0 * corner_e + corner_d)
    to_b = scaled * (2.0 * corner_a + 4.0 * corner_b + corner_e + 2.0 * corner_d)
    to_e = scaled * (2.0 * corner_a + corner_b + 4.0 * corner_e + 2.0 * corner_d)
    to_d = scaled * (corner_a + 2.0 * corner_b + 2.0 * corner_e + 4.0 * corner_d)
    total = jnp.pad(to_a, ((0, 1), (0, 1), (0, 0))) + jnp.pad(to_b, ((0, 1), (1, 0), (0, 0)))
    total = (
        total + jnp.pad(to_e, ((1, 0), (0, 1), (0, 0))) + jnp.pad(to_d, ((1, 0), (1, 0), (0, 0)))
    )
    return total


def contract(left, right):
    return lax.dot_general(
        left,
        right,
        (((0,), (0,)), ((), ())),
        precision=lax.Precision.HIGHEST,
        preferred_element_type=jnp.float32,
    )


def ring_gather(block, axis):
    count = lax.axis_size(axis)
    held = [block]
    for shift in range(1, count):
        held.append(lax.ppermute(block, axis, [(i, (i + shift) % count) for i in range(count)]))
    return jnp.concatenate(held, 1)


def direct_reduce_scatter(piece_of, axis):
    count = lax.axis_size(axis)
    me = lax.axis_index(axis)
    total = piece_of(me)
    for shift in range(1, count):
        total = total + lax.ppermute(
            piece_of((me + shift) % count), axis, [(i, (i + shift) % count) for i in range(count)]
        )
    return total


def local(snapshots, region_ids, conductivity):
    strip, width = region_ids.shape
    node_rows, group_cols = snapshots.shape
    side = lax.axis_size("c")
    tiles = lax.axis_size("mesh")
    field = snapshots.reshape(strip, width, group_cols)
    weight = weights_of(region_ids, conductivity)
    below = passed_along(field[0], "mesh", -1)
    total = element_terms(field, below, weight)
    carried = passed_along(total[strip, :width], "mesh", 1)
    inner = total[:strip, :width]
    panel = jnp.concatenate([inner[:1] + carried[None], inner[1:]], 0).reshape(
        node_rows, group_cols
    )
    rows = ring_gather(snapshots, "c")
    cols = ring_gather(panel, "r")
    partial_value = contract(rows, cols)
    me_r, me_c = lax.axis_index("r"), lax.axis_index("c")

    def piece_of(t):
        row_block = (me_c - t // side) % side
        col_block = (me_r - t % side) % side
        return lax.dynamic_slice(
            partial_value, (row_block * group_cols, col_block * group_cols), (group_cols, group_cols)
        )

    summed = direct_reduce_scatter(piece_of, "mesh")
    perm = []
    for c in range(side):
        for t in range(tiles):
            dest_c, dest_t = t // side, c + side * (t % side)
            perm.append((c * tiles + t, dest_c * tiles + dest_t))
    placed = lax.ppermute(summed, ("c", "mesh"), perm)
    total_nodes = node_rows * tiles
    return placed / math.sqrt(total_nodes)


def solution(mesh):
    snap = mesh.shape["snap"]
    side = math.isqrt(snap)
    grid = Mesh(
        mesh.devices.reshape(snap // side, side, mesh.shape["mesh"]), ("r", "c", "mesh")
    )
    return jax.shard_map(
        local,
        mesh=grid,
        in_specs=(P("mesh", ("r", "c")), P("mesh", None), P()),
        out_specs=P(("r", "c"), "mesh"),
        check_vma=False,
    )
```

```python
import math

import jax
import jax.numpy as jnp
from jax import lax
from jax.sharding import Mesh
from jax.sharding import PartitionSpec as P


def passed_along(value, axis, steps):
    count = lax.axis_size(axis)
    first, last = (max(0, -steps), min(count, count - steps))
    return lax.ppermute(value, axis, [(source, source + steps) for source in range(first, last)])


def weights_of(region_ids, conductivity):
    table = jnp.arange(conductivity.shape[0], dtype=jnp.int32)
    picked = jnp.where(
        region_ids[:, :, None] == table[None, None, :],
        conductivity[None, None, :],
        jnp.zeros((), conductivity.dtype),
    )
    return jnp.sum(picked, axis=-1) / 36.0


def element_terms(field, below, weight):
    lower = jnp.concatenate([field, below[None]], 0)
    padded = jnp.pad(lower, ((0, 0), (0, 1), (0, 0)))
    corner_a = padded[:-1, :-1]
    corner_b = padded[:-1, 1:]
    corner_e = padded[1:, :-1]
    corner_d = padded[1:, 1:]
    scaled = weight[:, :, None]
    to_a = scaled * (4.0 * corner_a + 2.0 * corner_b + 2.0 * corner_e + corner_d)
    to_b = scaled * (2.0 * corner_a + 4.0 * corner_b + corner_e + 2.0 * corner_d)
    to_e = scaled * (2.0 * corner_a + corner_b + 4.0 * corner_e + 2.0 * corner_d)
    to_d = scaled * (corner_a + 2.0 * corner_b + 2.0 * corner_e + 4.0 * corner_d)
    total = jnp.pad(to_a, ((0, 1), (0, 1), (0, 0))) + jnp.pad(to_b, ((0, 1), (1, 0), (0, 0)))
    total = (
        total + jnp.pad(to_e, ((1, 0), (0, 1), (0, 0))) + jnp.pad(to_d, ((1, 0), (1, 0), (0, 0)))
    )
    return total


def contract(left, right):
    return lax.dot_general(
        left,
        right,
        (((0,), (0,)), ((), ())),
        precision=lax.Precision.HIGH,
        preferred_element_type=jnp.float32,
    )


def ring_gather(block, axis):
    count = lax.axis_size(axis)
    held = [block]
    for shift in range(1, count):
        held.append(lax.ppermute(block, axis, [(i, (i + shift) % count) for i in range(count)]))
    return jnp.concatenate(held, 1)


def local(snapshots, region_ids, conductivity):
    strip, width = region_ids.shape
    node_rows, group_cols = snapshots.shape
    side = lax.axis_size("c")
    tiles = lax.axis_size("mesh")
    field = snapshots.reshape(strip, width, group_cols)
    weight = weights_of(region_ids, conductivity)
    below = passed_along(field[0], "mesh", -1)
    total = element_terms(field, below, weight)
    carried = passed_along(total[strip, :width], "mesh", 1)
    inner = total[:strip, :width]
    panel = jnp.concatenate([inner[:1] + carried[None], inner[1:]], 0).reshape(
        node_rows, group_cols
    )
    rows = ring_gather(snapshots, "c")
    cols = ring_gather(panel, "r")
    partial_value = contract(rows, cols)
    me_r, me_c, me_t = lax.axis_index("r"), lax.axis_index("c"), lax.axis_index("mesh")

    def piece_of(j):
        row_block = (me_c - j // side) % side
        col_block = (me_r - j % side) % side
        return lax.dynamic_slice(
            partial_value, (row_block * group_cols, col_block * group_cols), (group_cols, group_cols)
        )

    placed = None
    for step in range(tiles):
        perm = []
        for c in range(side):
            for t in range(tiles):
                j = (t + step) % tiles
                perm.append((c * tiles + t, (j // side) * tiles + c + side * (j % side)))
        moved = lax.ppermute(piece_of((me_t + step) % tiles), ("c", "mesh"), perm)
        placed = moved if placed is None else placed + moved
    total_nodes = node_rows * tiles
    return placed / math.sqrt(total_nodes)


def solution(mesh):
    snap = mesh.shape["snap"]
    side = math.isqrt(snap)
    grid = Mesh(
        mesh.devices.reshape(snap // side, side, mesh.shape["mesh"]), ("r", "c", "mesh")
    )
    return jax.shard_map(
        local,
        mesh=grid,
        in_specs=(P("mesh", ("r", "c")), P("mesh", None), P()),
        out_specs=P(("r", "c"), "mesh"),
        check_vma=False,
    )
```

```python
import math

import jax
import jax.numpy as jnp
from jax import lax
from jax.sharding import Mesh
from jax.sharding import PartitionSpec as P


def passed_along(value, axis, steps):
    count = lax.axis_size(axis)
    first, last = (max(0, -steps), min(count, count - steps))
    return lax.ppermute(value, axis, [(source, source + steps) for source in range(first, last)])


def weights_of(region_ids, conductivity):
    table = jnp.arange(conductivity.shape[0], dtype=jnp.int32)
    picked = jnp.where(
        region_ids[:, :, None] == table[None, None, :],
        conductivity[None, None, :],
        jnp.zeros((), conductivity.dtype),
    )
    return jnp.sum(picked, axis=-1) / 36.0


def element_terms(field, below, weight):
    lower = jnp.concatenate([field, below[None]], 0)
    padded = jnp.pad(lower, ((0, 0), (0, 1), (0, 0)))
    corner_a = padded[:-1, :-1]
    corner_b = padded[:-1, 1:]
    corner_e = padded[1:, :-1]
    corner_d = padded[1:, 1:]
    scaled = weight[:, :, None]
    to_a = scaled * (4.0 * corner_a + 2.0 * corner_b + 2.0 * corner_e + corner_d)
    to_b = scaled * (2.0 * corner_a + 4.0 * corner_b + corner_e + 2.0 * corner_d)
    to_e = scaled * (2.0 * corner_a + corner_b + 4.0 * corner_e + 2.0 * corner_d)
    to_d = scaled * (corner_a + 2.0 * corner_b + 2.0 * corner_e + 4.0 * corner_d)
    total = jnp.pad(to_a, ((0, 1), (0, 1), (0, 0))) + jnp.pad(to_b, ((0, 1), (1, 0), (0, 0)))
    total = (
        total + jnp.pad(to_e, ((1, 0), (0, 1), (0, 0))) + jnp.pad(to_d, ((1, 0), (1, 0), (0, 0)))
    )
    return total


def contract(left, right):
    return lax.dot_general(
        left,
        right,
        (((0,), (0,)), ((), ())),
        precision=lax.Precision.HIGH,
        preferred_element_type=jnp.float32,
    )


def pairs(count, to):
    return [(i, to(i)) for i in range(count)]


def square_gather(block, axis):
    count, half = lax.axis_size(axis), block.shape[0] // 2
    from_x = lax.ppermute(block, axis, pairs(count, lambda i: i ^ 1))
    from_z = lax.ppermute(block, axis, pairs(count, lambda i: i ^ 2))
    corner = jnp.concatenate(
        [
            lax.ppermute(from_x[:half], axis, pairs(count, lambda i: i ^ 2)),
            lax.ppermute(from_z[half:], axis, pairs(count, lambda i: i ^ 1)),
        ],
        0,
    )
    return jnp.concatenate([block, from_x, from_z, corner], 1)


def ring_gather(block, axis):
    count, half = lax.axis_size(axis), block.shape[0] // 2
    from_left = lax.ppermute(block, axis, pairs(count, lambda i: (i + 1) % count))
    from_right = lax.ppermute(block, axis, pairs(count, lambda i: (i - 1) % count))
    far = jnp.concatenate(
        [
            lax.ppermute(from_left[:half], axis, pairs(count, lambda i: (i + 1) % count)),
            lax.ppermute(from_right[half:], axis, pairs(count, lambda i: (i - 1) % count)),
        ],
        0,
    )
    return jnp.concatenate([block, from_left, far, from_right], 1)


def local(snapshots, region_ids, conductivity):
    strip, width = region_ids.shape
    node_rows, group_cols = snapshots.shape
    side = lax.axis_size("c")
    tiles = lax.axis_size("mesh")
    field = snapshots.reshape(strip, width, group_cols)
    weight = weights_of(region_ids, conductivity)
    below = passed_along(field[0], "mesh", -1)
    total = element_terms(field, below, weight)
    carried = passed_along(total[strip, :width], "mesh", 1)
    inner = total[:strip, :width]
    panel = jnp.concatenate([inner[:1] + carried[None], inner[1:]], 0).reshape(
        node_rows, group_cols
    )
    rows = square_gather(snapshots, "c")
    cols = ring_gather(panel, "r")
    partial_value = contract(rows, cols)
    me_r, me_c, me_t = lax.axis_index("r"), lax.axis_index("c"), lax.axis_index("mesh")

    def piece_of(j):
        row_block = jnp.bitwise_xor(me_c, j // side)
        col_block = (me_r - j % side) % side
        return lax.dynamic_slice(
            partial_value, (row_block * group_cols, col_block * group_cols), (group_cols, group_cols)
        )

    placed = None
    for step in range(tiles):
        perm = []
        for c in range(side):
            for t in range(tiles):
                j = (t + step) % tiles
                perm.append((c * tiles + t, (j // side) * tiles + c + side * (j % side)))
        moved = lax.ppermute(piece_of((me_t + step) % tiles), ("c", "mesh"), perm)
        placed = moved if placed is None else placed + moved
    total_nodes = node_rows * tiles
    return placed / math.sqrt(total_nodes)


def solution(mesh):
    snap = mesh.shape["snap"]
    side = math.isqrt(snap)
    grid = Mesh(
        mesh.devices.reshape(snap // side, side, mesh.shape["mesh"]), ("r", "c", "mesh")
    )
    return jax.shard_map(
        local,
        mesh=grid,
        in_specs=(P("mesh", ("r", "c")), P("mesh", None), P()),
        out_specs=P(("r", "c"), "mesh"),
        check_vma=False,
    )
```

```python
import functools
import math

import jax
import jax.numpy as jnp
from jax import lax
from jax.experimental import pallas as pl
from jax.experimental.pallas import tpu as pltpu
from jax.sharding import Mesh
from jax.sharding import PartitionSpec as P


def passed_along(value, axis, steps):
    count = lax.axis_size(axis)
    first, last = (max(0, -steps), min(count, count - steps))
    return lax.ppermute(value, axis, [(source, source + steps) for source in range(first, last)])


def weights_of(region_ids, conductivity):
    table = jnp.arange(conductivity.shape[0], dtype=jnp.int32)
    picked = jnp.where(
        region_ids[:, :, None] == table[None, None, :],
        conductivity[None, None, :],
        jnp.zeros((), conductivity.dtype),
    )
    return jnp.sum(picked, axis=-1) / 36.0


def element_terms(field, below, weight):
    lower = jnp.concatenate([field, below[None]], 0)
    padded = jnp.pad(lower, ((0, 0), (0, 1), (0, 0)))
    corner_a = padded[:-1, :-1]
    corner_b = padded[:-1, 1:]
    corner_e = padded[1:, :-1]
    corner_d = padded[1:, 1:]
    scaled = weight[:, :, None]
    to_a = scaled * (4.0 * corner_a + 2.0 * corner_b + 2.0 * corner_e + corner_d)
    to_b = scaled * (2.0 * corner_a + 4.0 * corner_b + corner_e + 2.0 * corner_d)
    to_e = scaled * (2.0 * corner_a + corner_b + 4.0 * corner_e + 2.0 * corner_d)
    to_d = scaled * (corner_a + 2.0 * corner_b + 2.0 * corner_e + 4.0 * corner_d)
    total = jnp.pad(to_a, ((0, 1), (0, 1), (0, 0))) + jnp.pad(to_b, ((0, 1), (1, 0), (0, 0)))
    total = (
        total + jnp.pad(to_e, ((1, 0), (0, 1), (0, 0))) + jnp.pad(to_d, ((1, 0), (1, 0), (0, 0)))
    )
    return total


def contract(left, right):
    return lax.dot_general(
        left,
        right,
        (((0,), (0,)), ((), ())),
        precision=lax.Precision.HIGH,
        preferred_element_type=jnp.float32,
    )


def pairs(count, to):
    return [(i, to(i)) for i in range(count)]


def square_gather(block, axis):
    count, half = lax.axis_size(axis), block.shape[0] // 2
    from_x = lax.ppermute(block, axis, pairs(count, lambda i: i ^ 1))
    from_z = lax.ppermute(block, axis, pairs(count, lambda i: i ^ 2))
    corner = jnp.concatenate(
        [
            lax.ppermute(from_x[:half], axis, pairs(count, lambda i: i ^ 2)),
            lax.ppermute(from_z[half:], axis, pairs(count, lambda i: i ^ 1)),
        ],
        0,
    )
    return jnp.concatenate([block, from_x, from_z, corner], 1)


def ring_gather(block, axis):
    count, half = lax.axis_size(axis), block.shape[0] // 2
    from_left = lax.ppermute(block, axis, pairs(count, lambda i: (i + 1) % count))
    from_right = lax.ppermute(block, axis, pairs(count, lambda i: (i - 1) % count))
    far = jnp.concatenate(
        [
            lax.ppermute(from_left[:half], axis, pairs(count, lambda i: (i + 1) % count)),
            lax.ppermute(from_right[half:], axis, pairs(count, lambda i: (i - 1) % count)),
        ],
        0,
    )
    return jnp.concatenate([block, from_left, far, from_right], 1)


def two_bit_xor(a, b):
    both = (a % 2) * (b % 2) + 2 * ((a // 2) * (b // 2))
    return a + b - 2 * both


def owners_kernel(side, tiles, part_ref, out_ref, slots, send_sems, recv_sems):
    me_r, me_c, me_t = lax.axis_index("r"), lax.axis_index("c"), lax.axis_index("mesh")
    width = out_ref.shape[0]
    mine = (me_t % side) == me_c
    sends = []
    for j in range(tiles):
        row_block = two_bit_xor(me_c, j // side)
        col_block = (me_r - j % side + side) % side
        dest_t = me_c + side * (j % side)
        to_self = jnp.logical_and(me_c == j // side, dest_t == me_t)
        copy = pltpu.make_async_remote_copy(
            src_ref=part_ref.at[
                pl.ds(pl.multiple_of(row_block * width, width), width),
                pl.ds(pl.multiple_of(col_block * width, width), width),
            ],
            dst_ref=slots.at[me_t],
            send_sem=send_sems.at[j],
            recv_sem=recv_sems.at[me_t],
            device_id=(me_r, j // side, dest_t),
            device_id_type=pl.DeviceIdType.MESH,
        )
        sends.append((copy, to_self, row_block, col_block))

        @pl.when(jnp.logical_not(to_self))
        def _():
            copy.start()

    for j, (copy, to_self, row_block, col_block) in enumerate(sends):

        @pl.when(to_self)
        def _():
            slots[me_t] = part_ref[
                pl.ds(pl.multiple_of(row_block * width, width), width),
                pl.ds(pl.multiple_of(col_block * width, width), width),
            ]

    for source in range(tiles):
        arrival = pltpu.make_async_remote_copy(
            src_ref=slots.at[source],
            dst_ref=slots.at[source],
            send_sem=send_sems.at[source],
            recv_sem=recv_sems.at[source],
            device_id=(me_r, me_c, me_t),
            device_id_type=pl.DeviceIdType.MESH,
        )

        @pl.when(jnp.logical_not(jnp.logical_and(mine, me_t == source)))
        def _():
            arrival.wait_recv()

    for copy, to_self, _, _ in sends:

        @pl.when(jnp.logical_not(to_self))
        def _():
            copy.wait_send()

    acc = slots[0]
    for source in range(1, tiles):
        acc = acc + slots[source]
    out_ref[...] = acc


def scatter_to_owners(partial_value, side, tiles):
    width = partial_value.shape[0] // side
    return pl.pallas_call(
        functools.partial(owners_kernel, side, tiles),
        out_shape=jax.ShapeDtypeStruct((width, width), jnp.float32),
        in_specs=[pl.BlockSpec(memory_space=pltpu.VMEM)],
        out_specs=pl.BlockSpec(memory_space=pltpu.VMEM),
        scratch_shapes=[
            pltpu.VMEM((tiles, width, width), jnp.float32),
            pltpu.SemaphoreType.DMA((tiles,)),
            pltpu.SemaphoreType.DMA((tiles,)),
        ],
        compiler_params=pltpu.CompilerParams(has_side_effects=True),
    )(partial_value)


def local(snapshots, region_ids, conductivity):
    strip, width = region_ids.shape
    node_rows, group_cols = snapshots.shape
    side = lax.axis_size("c")
    tiles = lax.axis_size("mesh")
    field = snapshots.reshape(strip, width, group_cols)
    weight = weights_of(region_ids, conductivity)
    below = passed_along(field[0], "mesh", -1)
    total = element_terms(field, below, weight)
    carried = passed_along(total[strip, :width], "mesh", 1)
    inner = total[:strip, :width]
    panel = jnp.concatenate([inner[:1] + carried[None], inner[1:]], 0).reshape(
        node_rows, group_cols
    )
    rows = square_gather(snapshots, "c")
    cols = ring_gather(panel, "r")
    partial_value = contract(rows, cols)
    placed = scatter_to_owners(partial_value, side, tiles)
    total_nodes = node_rows * tiles
    return placed / math.sqrt(total_nodes)


def solution(mesh):
    snap = mesh.shape["snap"]
    side = math.isqrt(snap)
    grid = Mesh(
        mesh.devices.reshape(snap // side, side, mesh.shape["mesh"]), ("r", "c", "mesh")
    )
    return jax.shard_map(
        local,
        mesh=grid,
        in_specs=(P("mesh", ("r", "c")), P("mesh", None), P()),
        out_specs=P(("r", "c"), "mesh"),
        check_vma=False,
    )
```

```python
import functools
import math

import jax
import jax.numpy as jnp
from jax import lax
from jax.experimental import pallas as pl
from jax.experimental.pallas import tpu as pltpu
from jax.sharding import Mesh
from jax.sharding import PartitionSpec as P


def passed_along(value, axis, steps):
    count = lax.axis_size(axis)
    first, last = (max(0, -steps), min(count, count - steps))
    return lax.ppermute(value, axis, [(source, source + steps) for source in range(first, last)])


def weights_of(region_ids, conductivity):
    table = jnp.arange(conductivity.shape[0], dtype=jnp.int32)
    picked = jnp.where(
        region_ids[:, :, None] == table[None, None, :],
        conductivity[None, None, :],
        jnp.zeros((), conductivity.dtype),
    )
    return jnp.sum(picked, axis=-1) / 36.0


def element_terms(field, below, weight):
    lower = jnp.concatenate([field, below[None]], 0)
    padded = jnp.pad(lower, ((0, 0), (0, 1), (0, 0)))
    corner_a = padded[:-1, :-1]
    corner_b = padded[:-1, 1:]
    corner_e = padded[1:, :-1]
    corner_d = padded[1:, 1:]
    scaled = weight[:, :, None]
    to_a = scaled * (4.0 * corner_a + 2.0 * corner_b + 2.0 * corner_e + corner_d)
    to_b = scaled * (2.0 * corner_a + 4.0 * corner_b + corner_e + 2.0 * corner_d)
    to_e = scaled * (2.0 * corner_a + corner_b + 4.0 * corner_e + 2.0 * corner_d)
    to_d = scaled * (corner_a + 2.0 * corner_b + 2.0 * corner_e + 4.0 * corner_d)
    total = jnp.pad(to_a, ((0, 1), (0, 1), (0, 0))) + jnp.pad(to_b, ((0, 1), (1, 0), (0, 0)))
    total = (
        total + jnp.pad(to_e, ((1, 0), (0, 1), (0, 0))) + jnp.pad(to_d, ((1, 0), (1, 0), (0, 0)))
    )
    return total


def contract(left, right):
    return lax.dot_general(
        left,
        right,
        (((0,), (0,)), ((), ())),
        precision=lax.Precision.HIGH,
        preferred_element_type=jnp.float32,
    )


def pairs(count, to):
    return [(i, to(i)) for i in range(count)]


def square_gather(block, axis):
    count, half = lax.axis_size(axis), block.shape[0] // 2
    from_x = lax.ppermute(block, axis, pairs(count, lambda i: i ^ 1))
    from_z = lax.ppermute(block, axis, pairs(count, lambda i: i ^ 2))
    corner = jnp.concatenate(
        [
            lax.ppermute(from_x[:half], axis, pairs(count, lambda i: i ^ 2)),
            lax.ppermute(from_z[half:], axis, pairs(count, lambda i: i ^ 1)),
        ],
        0,
    )
    return jnp.concatenate([block, from_x, from_z, corner], 1)


def ring_gather(block, axis):
    count, half = lax.axis_size(axis), block.shape[0] // 2
    from_left = lax.ppermute(block, axis, pairs(count, lambda i: (i + 1) % count))
    from_right = lax.ppermute(block, axis, pairs(count, lambda i: (i - 1) % count))
    far = jnp.concatenate(
        [
            lax.ppermute(from_left[:half], axis, pairs(count, lambda i: (i + 1) % count)),
            lax.ppermute(from_right[half:], axis, pairs(count, lambda i: (i - 1) % count)),
        ],
        0,
    )
    return jnp.concatenate([block, from_left, far, from_right], 1)


def two_bit_xor(a, b):
    both = (a % 2) * (b % 2) + 2 * ((a // 2) * (b // 2))
    return a + b - 2 * both


def owners_kernel(side, tiles, part_ref, out_ref, slots, send_sems, recv_sems):
    me_r, me_c, me_t = lax.axis_index("r"), lax.axis_index("c"), lax.axis_index("mesh")
    width = out_ref.shape[0]
    mine = (me_t % side) == me_c
    sends = []
    for j in range(tiles):
        row_block = two_bit_xor(me_c, j // side)
        col_block = (me_r - j % side + side) % side
        dest_t = me_c + side * (j % side)
        to_self = jnp.logical_and(me_c == j // side, dest_t == me_t)
        copy = pltpu.make_async_remote_copy(
            src_ref=part_ref.at[
                pl.ds(pl.multiple_of(row_block * width, width), width),
                pl.ds(pl.multiple_of(col_block * width, width), width),
            ],
            dst_ref=slots.at[me_t],
            send_sem=send_sems.at[j],
            recv_sem=recv_sems.at[me_t],
            device_id=(me_r, j // side, dest_t),
            device_id_type=pl.DeviceIdType.MESH,
        )
        sends.append((copy, to_self, row_block, col_block))

        @pl.when(jnp.logical_not(to_self))
        def _():
            copy.start()

    for j, (copy, to_self, row_block, col_block) in enumerate(sends):

        @pl.when(to_self)
        def _():
            slots[me_t] = part_ref[
                pl.ds(pl.multiple_of(row_block * width, width), width),
                pl.ds(pl.multiple_of(col_block * width, width), width),
            ]

    for source in range(tiles):
        arrival = pltpu.make_async_remote_copy(
            src_ref=slots.at[source],
            dst_ref=slots.at[source],
            send_sem=send_sems.at[source],
            recv_sem=recv_sems.at[source],
            device_id=(me_r, me_c, me_t),
            device_id_type=pl.DeviceIdType.MESH,
        )

        @pl.when(jnp.logical_not(jnp.logical_and(mine, me_t == source)))
        def _():
            arrival.wait_recv()

    for copy, to_self, _, _ in sends:

        @pl.when(jnp.logical_not(to_self))
        def _():
            copy.wait_send()

    acc = slots[0]
    for source in range(1, tiles):
        acc = acc + slots[source]
    out_ref[...] = acc


def scatter_to_owners(partial_value, side, tiles):
    width = partial_value.shape[0] // side
    return pl.pallas_call(
        functools.partial(owners_kernel, side, tiles),
        out_shape=jax.ShapeDtypeStruct((width, width), jnp.float32),
        in_specs=[pl.BlockSpec(memory_space=pltpu.VMEM)],
        out_specs=pl.BlockSpec(memory_space=pltpu.VMEM),
        scratch_shapes=[
            pltpu.VMEM((tiles, width, width), jnp.float32),
            pltpu.SemaphoreType.DMA((tiles,)),
            pltpu.SemaphoreType.DMA((tiles,)),
        ],
        compiler_params=pltpu.CompilerParams(has_side_effects=True),
    )(partial_value)


def gather_kernel(a_ref, b_ref, rows_ref, cols_ref, send_sems, recv_sems):
    me_r, me_c, me_t = lax.axis_index("r"), lax.axis_index("c"), lax.axis_index("mesh")
    count = lax.axis_size("r")
    half = a_ref.shape[0] // 2
    low, high = pl.ds(0, half), pl.ds(half, half)
    x_mate = (me_r, me_c + 1 - 2 * (me_c % 2), me_t)
    z_mate = (me_r, (me_c + 2) % 4, me_t)
    right = ((me_r + 1) % count, me_c, me_t)
    left = ((me_r + count - 1) % count, me_c, me_t)
    rows_ref[0] = a_ref[...]
    cols_ref[0] = b_ref[...]

    def copy(index, src, dst, device):
        return pltpu.make_async_remote_copy(
            src_ref=src,
            dst_ref=dst,
            send_sem=send_sems.at[index],
            recv_sem=recv_sems.at[index],
            device_id=device,
            device_id_type=pl.DeviceIdType.MESH,
        )

    first = [
        copy(0, a_ref.at[low], rows_ref.at[1, low], x_mate),
        copy(1, a_ref.at[high], rows_ref.at[2, high], z_mate),
        copy(2, b_ref.at[low], cols_ref.at[1, low], right),
        copy(3, b_ref.at[high], cols_ref.at[3, high], left),
    ]
    second = [
        copy(4, a_ref.at[high], rows_ref.at[1, high], x_mate),
        copy(5, a_ref.at[low], rows_ref.at[2, low], z_mate),
        copy(6, b_ref.at[high], cols_ref.at[1, high], right),
        copy(7, b_ref.at[low], cols_ref.at[3, low], left),
    ]
    for one in first + second:
        one.start()
    relays = [
        copy(8, rows_ref.at[1, low], rows_ref.at[3, low], z_mate),
        copy(9, rows_ref.at[2, high], rows_ref.at[3, high], x_mate),
        copy(10, cols_ref.at[1, low], cols_ref.at[2, low], right),
        copy(11, cols_ref.at[3, high], cols_ref.at[2, high], left),
    ]
    for arrived, relay in zip(first, relays):
        arrived.wait_recv()
        relay.start()
    for one in second + relays:
        one.wait_recv()
    for one in first + second + relays:
        one.wait_send()


def gather_both(snapshots, panel):
    node_rows, group_cols = snapshots.shape
    stack = jax.ShapeDtypeStruct((4, node_rows, group_cols), jnp.float32)
    return pl.pallas_call(
        gather_kernel,
        out_shape=(stack, stack),
        in_specs=[pl.BlockSpec(memory_space=pltpu.VMEM)] * 2,
        out_specs=(pl.BlockSpec(memory_space=pltpu.VMEM),) * 2,
        scratch_shapes=[pltpu.SemaphoreType.DMA((12,)), pltpu.SemaphoreType.DMA((12,))],
        compiler_params=pltpu.CompilerParams(
            has_side_effects=True, vmem_limit_bytes=48 * 1024 * 1024
        ),
    )(snapshots, panel)


def local(snapshots, region_ids, conductivity):
    strip, width = region_ids.shape
    node_rows, group_cols = snapshots.shape
    side = lax.axis_size("c")
    tiles = lax.axis_size("mesh")
    field = snapshots.reshape(strip, width, group_cols)
    weight = weights_of(region_ids, conductivity)
    below = passed_along(field[0], "mesh", -1)
    total = element_terms(field, below, weight)
    carried = passed_along(total[strip, :width], "mesh", 1)
    inner = total[:strip, :width]
    panel = jnp.concatenate([inner[:1] + carried[None], inner[1:]], 0).reshape(
        node_rows, group_cols
    )
    rows, cols = gather_both(snapshots, panel)
    partial_value = lax.dot_general(
        rows,
        cols,
        (((1,), (1,)), ((), ())),
        precision=lax.Precision.HIGH,
        preferred_element_type=jnp.float32,
    ).reshape(side * group_cols, side * group_cols)
    placed = scatter_to_owners(partial_value, side, tiles)
    total_nodes = node_rows * tiles
    return placed / math.sqrt(total_nodes)


def solution(mesh):
    snap = mesh.shape["snap"]
    side = math.isqrt(snap)
    grid = Mesh(
        mesh.devices.reshape(snap // side, side, mesh.shape["mesh"]), ("r", "c", "mesh")
    )
    return jax.shard_map(
        local,
        mesh=grid,
        in_specs=(P("mesh", ("r", "c")), P("mesh", None), P()),
        out_specs=P(("r", "c"), "mesh"),
        check_vma=False,
    )
```

```python
import functools
import math

import jax
import jax.numpy as jnp
from jax import lax
from jax.experimental import pallas as pl
from jax.experimental.pallas import tpu as pltpu
from jax.sharding import Mesh
from jax.sharding import PartitionSpec as P


def passed_along(value, axis, steps):
    count = lax.axis_size(axis)
    first, last = (max(0, -steps), min(count, count - steps))
    return lax.ppermute(value, axis, [(source, source + steps) for source in range(first, last)])


def weights_of(region_ids, conductivity):
    table = jnp.arange(conductivity.shape[0], dtype=jnp.int32)
    picked = jnp.where(
        region_ids[:, :, None] == table[None, None, :],
        conductivity[None, None, :],
        jnp.zeros((), conductivity.dtype),
    )
    return jnp.sum(picked, axis=-1) / 36.0


def element_terms(field, below, weight):
    lower = jnp.concatenate([field, below[None]], 0)
    padded = jnp.pad(lower, ((0, 0), (0, 1), (0, 0)))
    corner_a = padded[:-1, :-1]
    corner_b = padded[:-1, 1:]
    corner_e = padded[1:, :-1]
    corner_d = padded[1:, 1:]
    scaled = weight[:, :, None]
    to_a = scaled * (4.0 * corner_a + 2.0 * corner_b + 2.0 * corner_e + corner_d)
    to_b = scaled * (2.0 * corner_a + 4.0 * corner_b + corner_e + 2.0 * corner_d)
    to_e = scaled * (2.0 * corner_a + corner_b + 4.0 * corner_e + 2.0 * corner_d)
    to_d = scaled * (corner_a + 2.0 * corner_b + 2.0 * corner_e + 4.0 * corner_d)
    total = jnp.pad(to_a, ((0, 1), (0, 1), (0, 0))) + jnp.pad(to_b, ((0, 1), (1, 0), (0, 0)))
    total = (
        total + jnp.pad(to_e, ((1, 0), (0, 1), (0, 0))) + jnp.pad(to_d, ((1, 0), (1, 0), (0, 0)))
    )
    return total


def contract(left, right):
    return lax.dot_general(
        left,
        right,
        (((0,), (0,)), ((), ())),
        precision=lax.Precision.HIGH,
        preferred_element_type=jnp.float32,
    )


def pairs(count, to):
    return [(i, to(i)) for i in range(count)]


def square_gather(block, axis):
    count, half = lax.axis_size(axis), block.shape[0] // 2
    to_x, to_z = pairs(count, lambda i: i ^ 1), pairs(count, lambda i: i ^ 2)
    x_low = lax.ppermute(block[:half], axis, to_x)
    z_high = lax.ppermute(block[half:], axis, to_z)
    x_high = lax.ppermute(block[half:], axis, to_x)
    z_low = lax.ppermute(block[:half], axis, to_z)
    corner = [lax.ppermute(x_low, axis, to_z), lax.ppermute(z_high, axis, to_x)]
    return [block, [x_low, x_high], [z_low, z_high], corner]


def ring_gather(block, axis):
    count, half = lax.axis_size(axis), block.shape[0] // 2
    up = pairs(count, lambda i: (i + 1) % count)
    down = pairs(count, lambda i: (i - 1) % count)
    left_low = lax.ppermute(block[:half], axis, up)
    right_high = lax.ppermute(block[half:], axis, down)
    left_high = lax.ppermute(block[half:], axis, up)
    right_low = lax.ppermute(block[:half], axis, down)
    far = [lax.ppermute(left_low, axis, up), lax.ppermute(right_high, axis, down)]
    return [block, [left_low, left_high], far, [right_low, right_high]]


def block_product(row_block, col_block):
    if not isinstance(row_block, list):
        row_block = [row_block[: row_block.shape[0] // 2], row_block[row_block.shape[0] // 2 :]]
    if not isinstance(col_block, list):
        col_block = [col_block[: col_block.shape[0] // 2], col_block[col_block.shape[0] // 2 :]]
    return contract(row_block[0], col_block[0]) + contract(row_block[1], col_block[1])


def two_bit_xor(a, b):
    both = (a % 2) * (b % 2) + 2 * ((a // 2) * (b // 2))
    return a + b - 2 * both


def owners_kernel(side, tiles, part_ref, out_ref, slots, send_sems, recv_sems):
    me_r, me_c, me_t = lax.axis_index("r"), lax.axis_index("c"), lax.axis_index("mesh")
    width = out_ref.shape[0]
    mine = (me_t % side) == me_c
    sends = []
    for j in range(tiles):
        row_block = two_bit_xor(me_c, j // side)
        col_block = (me_r - j % side + side) % side
        dest_t = me_c + side * (j % side)
        to_self = jnp.logical_and(me_c == j // side, dest_t == me_t)
        copy = pltpu.make_async_remote_copy(
            src_ref=part_ref.at[
                pl.ds(pl.multiple_of(row_block * width, width), width),
                pl.ds(pl.multiple_of(col_block * width, width), width),
            ],
            dst_ref=slots.at[me_t],
            send_sem=send_sems.at[j],
            recv_sem=recv_sems.at[me_t],
            device_id=(me_r, j // side, dest_t),
            device_id_type=pl.DeviceIdType.MESH,
        )
        sends.append((copy, to_self, row_block, col_block))

        @pl.when(jnp.logical_not(to_self))
        def _():
            copy.start()

    for j, (copy, to_self, row_block, col_block) in enumerate(sends):

        @pl.when(to_self)
        def _():
            slots[me_t] = part_ref[
                pl.ds(pl.multiple_of(row_block * width, width), width),
                pl.ds(pl.multiple_of(col_block * width, width), width),
            ]

    for source in range(tiles):
        arrival = pltpu.make_async_remote_copy(
            src_ref=slots.at[source],
            dst_ref=slots.at[source],
            send_sem=send_sems.at[source],
            recv_sem=recv_sems.at[source],
            device_id=(me_r, me_c, me_t),
            device_id_type=pl.DeviceIdType.MESH,
        )

        @pl.when(jnp.logical_not(jnp.logical_and(mine, me_t == source)))
        def _():
            arrival.wait_recv()

    for copy, to_self, _, _ in sends:

        @pl.when(jnp.logical_not(to_self))
        def _():
            copy.wait_send()

    acc = slots[0]
    for source in range(1, tiles):
        acc = acc + slots[source]
    out_ref[...] = acc


def scatter_to_owners(partial_value, side, tiles):
    width = partial_value.shape[0] // side
    return pl.pallas_call(
        functools.partial(owners_kernel, side, tiles),
        out_shape=jax.ShapeDtypeStruct((width, width), jnp.float32),
        in_specs=[pl.BlockSpec(memory_space=pltpu.VMEM)],
        out_specs=pl.BlockSpec(memory_space=pltpu.VMEM),
        scratch_shapes=[
            pltpu.VMEM((tiles, width, width), jnp.float32),
            pltpu.SemaphoreType.DMA((tiles,)),
            pltpu.SemaphoreType.DMA((tiles,)),
        ],
        compiler_params=pltpu.CompilerParams(has_side_effects=True),
    )(partial_value)


def local(snapshots, region_ids, conductivity):
    strip, width = region_ids.shape
    node_rows, group_cols = snapshots.shape
    side = lax.axis_size("c")
    tiles = lax.axis_size("mesh")
    field = snapshots.reshape(strip, width, group_cols)
    weight = weights_of(region_ids, conductivity)
    below = passed_along(field[0], "mesh", -1)
    total = element_terms(field, below, weight)
    carried = passed_along(total[strip, :width], "mesh", 1)
    inner = total[:strip, :width]
    panel = jnp.concatenate([inner[:1] + carried[None], inner[1:]], 0).reshape(
        node_rows, group_cols
    )
    rows = square_gather(snapshots, "c")
    cols = ring_gather(panel, "r")
    partial_value = jnp.concatenate(
        [jnp.concatenate([block_product(a, b) for b in cols], 1) for a in rows], 0
    )
    placed = scatter_to_owners(partial_value, side, tiles)
    total_nodes = node_rows * tiles
    return placed / math.sqrt(total_nodes)


def solution(mesh):
    snap = mesh.shape["snap"]
    side = math.isqrt(snap)
    grid = Mesh(
        mesh.devices.reshape(snap // side, side, mesh.shape["mesh"]), ("r", "c", "mesh")
    )
    return jax.shard_map(
        local,
        mesh=grid,
        in_specs=(P("mesh", ("r", "c")), P("mesh", None), P()),
        out_specs=P(("r", "c"), "mesh"),
        check_vma=False,
    )
```

```python
import functools
import math

import jax
import jax.numpy as jnp
from jax import lax
from jax.experimental import pallas as pl
from jax.experimental.pallas import tpu as pltpu
from jax.sharding import Mesh
from jax.sharding import PartitionSpec as P


def passed_along(value, axis, steps):
    count = lax.axis_size(axis)
    first, last = (max(0, -steps), min(count, count - steps))
    return lax.ppermute(value, axis, [(source, source + steps) for source in range(first, last)])


def weights_of(region_ids, conductivity):
    table = jnp.arange(conductivity.shape[0], dtype=jnp.int32)
    picked = jnp.where(
        region_ids[:, :, None] == table[None, None, :],
        conductivity[None, None, :],
        jnp.zeros((), conductivity.dtype),
    )
    return jnp.sum(picked, axis=-1) / 36.0


def element_terms(field, below, weight):
    lower = jnp.concatenate([field, below[None]], 0)
    padded = jnp.pad(lower, ((0, 0), (0, 1), (0, 0)))
    corner_a = padded[:-1, :-1]
    corner_b = padded[:-1, 1:]
    corner_e = padded[1:, :-1]
    corner_d = padded[1:, 1:]
    scaled = weight[:, :, None]
    to_a = scaled * (4.0 * corner_a + 2.0 * corner_b + 2.0 * corner_e + corner_d)
    to_b = scaled * (2.0 * corner_a + 4.0 * corner_b + corner_e + 2.0 * corner_d)
    to_e = scaled * (2.0 * corner_a + corner_b + 4.0 * corner_e + 2.0 * corner_d)
    to_d = scaled * (corner_a + 2.0 * corner_b + 2.0 * corner_e + 4.0 * corner_d)
    total = jnp.pad(to_a, ((0, 1), (0, 1), (0, 0))) + jnp.pad(to_b, ((0, 1), (1, 0), (0, 0)))
    total = (
        total + jnp.pad(to_e, ((1, 0), (0, 1), (0, 0))) + jnp.pad(to_d, ((1, 0), (1, 0), (0, 0)))
    )
    return total


def contract(left, right):
    return lax.dot_general(
        left,
        right,
        (((0,), (0,)), ((), ())),
        precision=lax.Precision.HIGH,
        preferred_element_type=jnp.float32,
    )


def pairs(count, to):
    return [(i, to(i)) for i in range(count)]


def square_gather(block, axis):
    count, half = lax.axis_size(axis), block.shape[0] // 2
    to_x, to_z = pairs(count, lambda i: i ^ 1), pairs(count, lambda i: i ^ 2)
    x_low = lax.ppermute(block[:half], axis, to_x)
    z_high = lax.ppermute(block[half:], axis, to_z)
    x_high = lax.ppermute(block[half:], axis, to_x)
    z_low = lax.ppermute(block[:half], axis, to_z)
    corner = [lax.ppermute(x_low, axis, to_z), lax.ppermute(z_high, axis, to_x)]
    return [block, [x_low, x_high], [z_low, z_high], corner]


def ring_gather(block, axis):
    count, half = lax.axis_size(axis), block.shape[0] // 2
    up = pairs(count, lambda i: (i + 1) % count)
    down = pairs(count, lambda i: (i - 1) % count)
    left_low = lax.ppermute(block[:half], axis, up)
    right_high = lax.ppermute(block[half:], axis, down)
    left_high = lax.ppermute(block[half:], axis, up)
    right_low = lax.ppermute(block[:half], axis, down)
    far = [lax.ppermute(left_low, axis, up), lax.ppermute(right_high, axis, down)]
    return [block, [left_low, left_high], far, [right_low, right_high]]


def block_product(row_block, col_block):
    if not isinstance(row_block, list):
        row_block = [row_block[: row_block.shape[0] // 2], row_block[row_block.shape[0] // 2 :]]
    if not isinstance(col_block, list):
        col_block = [col_block[: col_block.shape[0] // 2], col_block[col_block.shape[0] // 2 :]]
    return contract(row_block[0], col_block[0]) + contract(row_block[1], col_block[1])


def two_bit_xor(a, b):
    both = (a % 2) * (b % 2) + 2 * ((a // 2) * (b // 2))
    return a + b - 2 * both


def owners_kernel(side, tiles, part_ref, out_ref, slots, send_sems, recv_sems):
    me_r, me_c, me_t = lax.axis_index("r"), lax.axis_index("c"), lax.axis_index("mesh")
    width = out_ref.shape[0]
    mine = (me_t % side) == me_c
    sends = []
    for j in range(tiles):
        row_block = two_bit_xor(me_c, j // side)
        col_block = (me_r - j % side + side) % side
        dest_t = me_c + side * (j % side)
        to_self = jnp.logical_and(me_c == j // side, dest_t == me_t)
        copy = pltpu.make_async_remote_copy(
            src_ref=part_ref.at[
                pl.ds(pl.multiple_of(row_block * width, width), width),
                pl.ds(pl.multiple_of(col_block * width, width), width),
            ],
            dst_ref=slots.at[me_t],
            send_sem=send_sems.at[j],
            recv_sem=recv_sems.at[me_t],
            device_id=(me_r, j // side, dest_t),
            device_id_type=pl.DeviceIdType.MESH,
        )
        sends.append((copy, to_self, row_block, col_block))

        @pl.when(jnp.logical_not(to_self))
        def _():
            copy.start()

    for j, (copy, to_self, row_block, col_block) in enumerate(sends):

        @pl.when(to_self)
        def _():
            slots[me_t] = part_ref[
                pl.ds(pl.multiple_of(row_block * width, width), width),
                pl.ds(pl.multiple_of(col_block * width, width), width),
            ]

    for source in range(tiles):
        arrival = pltpu.make_async_remote_copy(
            src_ref=slots.at[source],
            dst_ref=slots.at[source],
            send_sem=send_sems.at[source],
            recv_sem=recv_sems.at[source],
            device_id=(me_r, me_c, me_t),
            device_id_type=pl.DeviceIdType.MESH,
        )

        @pl.when(jnp.logical_not(jnp.logical_and(mine, me_t == source)))
        def _():
            arrival.wait_recv()

    for copy, to_self, _, _ in sends:

        @pl.when(jnp.logical_not(to_self))
        def _():
            copy.wait_send()

    acc = slots[0]
    for source in range(1, tiles):
        acc = acc + slots[source]
    out_ref[...] = acc


def scatter_to_owners(partial_value, side, tiles):
    width = partial_value.shape[0] // side
    return pl.pallas_call(
        functools.partial(owners_kernel, side, tiles),
        out_shape=jax.ShapeDtypeStruct((width, width), jnp.float32),
        in_specs=[pl.BlockSpec(memory_space=pltpu.VMEM)],
        out_specs=pl.BlockSpec(memory_space=pltpu.VMEM),
        scratch_shapes=[
            pltpu.VMEM((tiles, width, width), jnp.float32),
            pltpu.SemaphoreType.DMA((tiles,)),
            pltpu.SemaphoreType.DMA((tiles,)),
        ],
        compiler_params=pltpu.CompilerParams(has_side_effects=True),
    )(partial_value)


def local(snapshots, region_ids, conductivity):
    strip, width = region_ids.shape
    node_rows, group_cols = snapshots.shape
    side = lax.axis_size("c")
    tiles = lax.axis_size("mesh")
    field = snapshots.reshape(strip, width, group_cols)
    weight = weights_of(region_ids, conductivity)
    below = passed_along(field[0], "mesh", -1)
    total = element_terms(field, below, weight)
    carried = passed_along(total[strip, :width], "mesh", 1)
    inner = total[:strip, :width]
    panel = jnp.concatenate([inner[:1] + carried[None], inner[1:]], 0).reshape(
        node_rows, group_cols
    )
    rows = square_gather(panel, "c")
    cols = ring_gather(snapshots, "r")
    partial_value = jnp.concatenate(
        [jnp.concatenate([block_product(a, b) for b in cols], 1) for a in rows], 0
    )
    placed = scatter_to_owners(partial_value, side, tiles)
    total_nodes = node_rows * tiles
    return placed / math.sqrt(total_nodes)


def solution(mesh):
    snap = mesh.shape["snap"]
    side = math.isqrt(snap)
    grid = Mesh(
        mesh.devices.reshape(snap // side, side, mesh.shape["mesh"]), ("r", "c", "mesh")
    )
    return jax.shard_map(
        local,
        mesh=grid,
        in_specs=(P("mesh", ("r", "c")), P("mesh", None), P()),
        out_specs=P(("r", "c"), "mesh"),
        check_vma=False,
    )
```

```python
import functools
import math

import jax
import jax.numpy as jnp
from jax import lax
from jax.experimental import pallas as pl
from jax.experimental.pallas import tpu as pltpu
from jax.sharding import Mesh
from jax.sharding import PartitionSpec as P


def passed_along(value, axis, steps):
    count = lax.axis_size(axis)
    first, last = (max(0, -steps), min(count, count - steps))
    return lax.ppermute(value, axis, [(source, source + steps) for source in range(first, last)])


def weights_of(region_ids, conductivity):
    table = jnp.arange(conductivity.shape[0], dtype=jnp.int32)
    picked = jnp.where(
        region_ids[:, :, None] == table[None, None, :],
        conductivity[None, None, :],
        jnp.zeros((), conductivity.dtype),
    )
    return jnp.sum(picked, axis=-1) / 36.0


def element_terms(field, below, weight):
    lower = jnp.concatenate([field, below[None]], 0)
    padded = jnp.pad(lower, ((0, 0), (0, 1), (0, 0)))
    corner_a = padded[:-1, :-1]
    corner_b = padded[:-1, 1:]
    corner_e = padded[1:, :-1]
    corner_d = padded[1:, 1:]
    scaled = weight[:, :, None]
    to_a = scaled * (4.0 * corner_a + 2.0 * corner_b + 2.0 * corner_e + corner_d)
    to_b = scaled * (2.0 * corner_a + 4.0 * corner_b + corner_e + 2.0 * corner_d)
    to_e = scaled * (2.0 * corner_a + corner_b + 4.0 * corner_e + 2.0 * corner_d)
    to_d = scaled * (corner_a + 2.0 * corner_b + 2.0 * corner_e + 4.0 * corner_d)
    total = jnp.pad(to_a, ((0, 1), (0, 1), (0, 0))) + jnp.pad(to_b, ((0, 1), (1, 0), (0, 0)))
    total = (
        total + jnp.pad(to_e, ((1, 0), (0, 1), (0, 0))) + jnp.pad(to_d, ((1, 0), (1, 0), (0, 0)))
    )
    return total


def contract(left, right):
    return lax.dot_general(
        left,
        right,
        (((0,), (0,)), ((), ())),
        precision=lax.Precision.HIGH,
        preferred_element_type=jnp.float32,
    )


def pairs(count, to):
    return [(i, to(i)) for i in range(count)]


def square_gather(block, axis):
    count, half = lax.axis_size(axis), block.shape[0] // 2
    to_x, to_z = pairs(count, lambda i: i ^ 1), pairs(count, lambda i: i ^ 2)
    x_low = lax.ppermute(block[:half], axis, to_x)
    z_high = lax.ppermute(block[half:], axis, to_z)
    x_high = lax.ppermute(block[half:], axis, to_x)
    z_low = lax.ppermute(block[:half], axis, to_z)
    corner = [lax.ppermute(x_low, axis, to_z), lax.ppermute(z_high, axis, to_x)]
    return [block, [x_low, x_high], [z_low, z_high], corner]


def ring_gather(block, axis):
    count, half = lax.axis_size(axis), block.shape[0] // 2
    up = pairs(count, lambda i: (i + 1) % count)
    down = pairs(count, lambda i: (i - 1) % count)
    left_low = lax.ppermute(block[:half], axis, up)
    right_high = lax.ppermute(block[half:], axis, down)
    left_high = lax.ppermute(block[half:], axis, up)
    right_low = lax.ppermute(block[:half], axis, down)
    far = [lax.ppermute(left_low, axis, up), lax.ppermute(right_high, axis, down)]
    return [block, [left_low, left_high], far, [right_low, right_high]]


def block_product(row_block, col_block):
    if not isinstance(row_block, list):
        row_block = [row_block[: row_block.shape[0] // 2], row_block[row_block.shape[0] // 2 :]]
    if not isinstance(col_block, list):
        col_block = [col_block[: col_block.shape[0] // 2], col_block[col_block.shape[0] // 2 :]]
    return contract(row_block[0], col_block[0]) + contract(row_block[1], col_block[1])


def two_bit_xor(a, b):
    both = (a % 2) * (b % 2) + 2 * ((a // 2) * (b // 2))
    return a + b - 2 * both


def owners_kernel(side, tiles, part_ref, out_ref, slots, send_sems, recv_sems):
    me_r, me_c, me_t = lax.axis_index("r"), lax.axis_index("c"), lax.axis_index("mesh")
    halves = tiles // 2
    parity = me_t % 2
    sends = []
    for i in range(halves):
        j = 2 * i + parity
        dest_c = j // side
        dest_t = me_c + side * (j % side)
        to_self = jnp.logical_and(dest_c == me_c, dest_t == me_t)
        copy = pltpu.make_async_remote_copy(
            src_ref=part_ref.at[i],
            dst_ref=slots.at[me_t // 2],
            send_sem=send_sems.at[i],
            recv_sem=recv_sems.at[me_t // 2],
            device_id=(me_r, dest_c, dest_t),
            device_id_type=pl.DeviceIdType.MESH,
        )
        sends.append((copy, to_self, i))

        @pl.when(jnp.logical_not(to_self))
        def _():
            copy.start()

    for copy, to_self, i in sends:

        @pl.when(to_self)
        def _():
            slots[me_t // 2] = part_ref[i]

    incoming = (me_t // side) % 2
    mine = jnp.logical_and(me_t % side == me_c, parity == incoming)
    for source in range(halves):
        arrival = pltpu.make_async_remote_copy(
            src_ref=slots.at[source],
            dst_ref=slots.at[source],
            send_sem=send_sems.at[source],
            recv_sem=recv_sems.at[source],
            device_id=(me_r, me_c, me_t),
            device_id_type=pl.DeviceIdType.MESH,
        )

        @pl.when(jnp.logical_not(jnp.logical_and(mine, me_t // 2 == source)))
        def _():
            arrival.wait_recv()

    for copy, to_self, _ in sends:

        @pl.when(jnp.logical_not(to_self))
        def _():
            copy.wait_send()

    acc = slots[0]
    for source in range(1, halves):
        acc = acc + slots[source]
    out_ref[...] = acc


def scatter_to_owners(partial_value, side, tiles):
    width = partial_value.shape[0] // side
    me_r, me_c, me_t = lax.axis_index("r"), lax.axis_index("c"), lax.axis_index("mesh")
    parity = me_t % 2

    def piece_of(j):
        row_block = two_bit_xor(me_c, j // side)
        col_block = (me_r - j % side) % side
        return lax.dynamic_slice(partial_value, (row_block * width, col_block * width), (width, width))

    halves = tiles // 2
    kept = jnp.stack([piece_of(2 * i + parity) for i in range(halves)], 0)
    given = jnp.stack([piece_of(2 * i + 1 - parity) for i in range(halves)], 0)
    kept = kept + lax.ppermute(given, "mesh", pairs(tiles, lambda i: i ^ 1))
    return pl.pallas_call(
        functools.partial(owners_kernel, side, tiles),
        out_shape=jax.ShapeDtypeStruct((width, width), jnp.float32),
        in_specs=[pl.BlockSpec(memory_space=pltpu.VMEM)],
        out_specs=pl.BlockSpec(memory_space=pltpu.VMEM),
        scratch_shapes=[
            pltpu.VMEM((halves, width, width), jnp.float32),
            pltpu.SemaphoreType.DMA((halves,)),
            pltpu.SemaphoreType.DMA((halves,)),
        ],
        compiler_params=pltpu.CompilerParams(has_side_effects=True),
    )(kept)


def local(snapshots, region_ids, conductivity):
    strip, width = region_ids.shape
    node_rows, group_cols = snapshots.shape
    side = lax.axis_size("c")
    tiles = lax.axis_size("mesh")
    field = snapshots.reshape(strip, width, group_cols)
    weight = weights_of(region_ids, conductivity)
    below = passed_along(field[0], "mesh", -1)
    total = element_terms(field, below, weight)
    carried = passed_along(total[strip, :width], "mesh", 1)
    inner = total[:strip, :width]
    panel = jnp.concatenate([inner[:1] + carried[None], inner[1:]], 0).reshape(
        node_rows, group_cols
    )
    rows = square_gather(panel, "c")
    cols = ring_gather(snapshots, "r")
    partial_value = jnp.concatenate(
        [jnp.concatenate([block_product(a, b) for b in cols], 1) for a in rows], 0
    )
    placed = scatter_to_owners(partial_value, side, tiles)
    total_nodes = node_rows * tiles
    return placed / math.sqrt(total_nodes)


def solution(mesh):
    snap = mesh.shape["snap"]
    side = math.isqrt(snap)
    grid = Mesh(
        mesh.devices.reshape(snap // side, side, mesh.shape["mesh"]), ("r", "c", "mesh")
    )
    return jax.shard_map(
        local,
        mesh=grid,
        in_specs=(P("mesh", ("r", "c")), P("mesh", None), P()),
        out_specs=P(("r", "c"), "mesh"),
        check_vma=False,
    )
```

```python
import functools
import math

import jax
import jax.numpy as jnp
from jax import lax
from jax.experimental import pallas as pl
from jax.experimental.pallas import tpu as pltpu
from jax.sharding import Mesh
from jax.sharding import PartitionSpec as P


def passed_along(value, axis, steps):
    count = lax.axis_size(axis)
    first, last = (max(0, -steps), min(count, count - steps))
    return lax.ppermute(value, axis, [(source, source + steps) for source in range(first, last)])


def weights_of(region_ids, conductivity):
    table = jnp.arange(conductivity.shape[0], dtype=jnp.int32)
    picked = jnp.where(
        region_ids[:, :, None] == table[None, None, :],
        conductivity[None, None, :],
        jnp.zeros((), conductivity.dtype),
    )
    return jnp.sum(picked, axis=-1) / 36.0


def element_terms(field, below, weight):
    lower = jnp.concatenate([field, below[None]], 0)
    padded = jnp.pad(lower, ((0, 0), (0, 1), (0, 0)))
    corner_a = padded[:-1, :-1]
    corner_b = padded[:-1, 1:]
    corner_e = padded[1:, :-1]
    corner_d = padded[1:, 1:]
    scaled = weight[:, :, None]
    to_a = scaled * (4.0 * corner_a + 2.0 * corner_b + 2.0 * corner_e + corner_d)
    to_b = scaled * (2.0 * corner_a + 4.0 * corner_b + corner_e + 2.0 * corner_d)
    to_e = scaled * (2.0 * corner_a + corner_b + 4.0 * corner_e + 2.0 * corner_d)
    to_d = scaled * (corner_a + 2.0 * corner_b + 2.0 * corner_e + 4.0 * corner_d)
    total = jnp.pad(to_a, ((0, 1), (0, 1), (0, 0))) + jnp.pad(to_b, ((0, 1), (1, 0), (0, 0)))
    total = (
        total + jnp.pad(to_e, ((1, 0), (0, 1), (0, 0))) + jnp.pad(to_d, ((1, 0), (1, 0), (0, 0)))
    )
    return total


def contract(left, right):
    return lax.dot_general(
        left,
        right,
        (((0,), (0,)), ((), ())),
        precision=lax.Precision.HIGH,
        preferred_element_type=jnp.float32,
    )


def pairs(count, to):
    return [(i, to(i)) for i in range(count)]


def square_gather(block, axis):
    count, half = lax.axis_size(axis), block.shape[0] // 2
    to_x, to_z = pairs(count, lambda i: i ^ 1), pairs(count, lambda i: i ^ 2)
    x_low = lax.ppermute(block[:half], axis, to_x)
    z_high = lax.ppermute(block[half:], axis, to_z)
    x_high = lax.ppermute(block[half:], axis, to_x)
    z_low = lax.ppermute(block[:half], axis, to_z)
    corner = [lax.ppermute(x_low, axis, to_z), lax.ppermute(z_high, axis, to_x)]
    return [block, [x_low, x_high], [z_low, z_high], corner]


def ring_gather(block, axis):
    count, half = lax.axis_size(axis), block.shape[0] // 2
    up = pairs(count, lambda i: (i + 1) % count)
    down = pairs(count, lambda i: (i - 1) % count)
    left_low = lax.ppermute(block[:half], axis, up)
    right_high = lax.ppermute(block[half:], axis, down)
    left_high = lax.ppermute(block[half:], axis, up)
    right_low = lax.ppermute(block[:half], axis, down)
    far = [lax.ppermute(left_low, axis, up), lax.ppermute(right_high, axis, down)]
    return [block, [left_low, left_high], far, [right_low, right_high]]


def joined(block):
    return jnp.concatenate(block, 0) if isinstance(block, list) else block


def two_bit_xor(a, b):
    both = (a % 2) * (b % 2) + 2 * ((a // 2) * (b // 2))
    return a + b - 2 * both


def owners_kernel(side, tiles, part_ref, out_ref, slots, send_sems, recv_sems):
    me_r, me_c, me_t = lax.axis_index("r"), lax.axis_index("c"), lax.axis_index("mesh")
    halves = tiles // 2
    parity = me_t % 2
    sends = []
    for i in range(halves):
        j = 2 * i + parity
        dest_c = j // side
        dest_t = me_c + side * (j % side)
        to_self = jnp.logical_and(dest_c == me_c, dest_t == me_t)
        copy = pltpu.make_async_remote_copy(
            src_ref=part_ref.at[i],
            dst_ref=slots.at[me_t // 2],
            send_sem=send_sems.at[i],
            recv_sem=recv_sems.at[me_t // 2],
            device_id=(me_r, dest_c, dest_t),
            device_id_type=pl.DeviceIdType.MESH,
        )
        sends.append((copy, to_self, i))

        @pl.when(jnp.logical_not(to_self))
        def _():
            copy.start()

    for copy, to_self, i in sends:

        @pl.when(to_self)
        def _():
            slots[me_t // 2] = part_ref[i]

    incoming = (me_t // side) % 2
    mine = jnp.logical_and(me_t % side == me_c, parity == incoming)
    for source in range(halves):
        arrival = pltpu.make_async_remote_copy(
            src_ref=slots.at[source],
            dst_ref=slots.at[source],
            send_sem=send_sems.at[source],
            recv_sem=recv_sems.at[source],
            device_id=(me_r, me_c, me_t),
            device_id_type=pl.DeviceIdType.MESH,
        )

        @pl.when(jnp.logical_not(jnp.logical_and(mine, me_t // 2 == source)))
        def _():
            arrival.wait_recv()

    for copy, to_self, _ in sends:

        @pl.when(jnp.logical_not(to_self))
        def _():
            copy.wait_send()

    acc = slots[0]
    for source in range(1, halves):
        acc = acc + slots[source]
    out_ref[...] = acc


def scatter_to_owners(blocks, side, tiles):
    width = blocks.shape[-1]
    me_r, me_c, me_t = lax.axis_index("r"), lax.axis_index("c"), lax.axis_index("mesh")
    halves = tiles // 2
    index = jnp.arange(halves, dtype=jnp.int32)

    def pieces(parity):
        j = 2 * index + parity
        return blocks[two_bit_xor(me_c, j // side), (me_r - j % side) % side]

    parity = me_t % 2
    kept = pieces(parity) + lax.ppermute(pieces(1 - parity), "mesh", pairs(tiles, lambda i: i ^ 1))
    return pl.pallas_call(
        functools.partial(owners_kernel, side, tiles),
        out_shape=jax.ShapeDtypeStruct((width, width), jnp.float32),
        in_specs=[pl.BlockSpec(memory_space=pltpu.VMEM)],
        out_specs=pl.BlockSpec(memory_space=pltpu.VMEM),
        scratch_shapes=[
            pltpu.VMEM((halves, width, width), jnp.float32),
            pltpu.SemaphoreType.DMA((halves,)),
            pltpu.SemaphoreType.DMA((halves,)),
        ],
        compiler_params=pltpu.CompilerParams(has_side_effects=True),
    )(kept)


def local(snapshots, region_ids, conductivity):
    strip, width = region_ids.shape
    node_rows, group_cols = snapshots.shape
    side = lax.axis_size("c")
    tiles = lax.axis_size("mesh")
    field = snapshots.reshape(strip, width, group_cols)
    weight = weights_of(region_ids, conductivity)
    below = passed_along(field[0], "mesh", -1)
    total = element_terms(field, below, weight)
    carried = passed_along(total[strip, :width], "mesh", 1)
    inner = total[:strip, :width]
    panel = jnp.concatenate([inner[:1] + carried[None], inner[1:]], 0).reshape(
        node_rows, group_cols
    )
    rows = square_gather(panel, "c")
    cols = ring_gather(snapshots, "r")
    blocks = jnp.stack(
        [jnp.stack([contract(joined(a), joined(b)) for b in cols], 0) for a in rows], 0
    )
    placed = scatter_to_owners(blocks, side, tiles)
    total_nodes = node_rows * tiles
    return placed / math.sqrt(total_nodes)


def solution(mesh):
    snap = mesh.shape["snap"]
    side = math.isqrt(snap)
    grid = Mesh(
        mesh.devices.reshape(snap // side, side, mesh.shape["mesh"]), ("r", "c", "mesh")
    )
    return jax.shard_map(
        local,
        mesh=grid,
        in_specs=(P("mesh", ("r", "c")), P("mesh", None), P()),
        out_specs=P(("r", "c"), "mesh"),
        check_vma=False,
    )
```

```python
import functools
import math

import jax
import jax.numpy as jnp
from jax import lax
from jax.experimental import pallas as pl
from jax.experimental.pallas import tpu as pltpu
from jax.sharding import Mesh
from jax.sharding import PartitionSpec as P


def passed_along(value, axis, steps):
    count = lax.axis_size(axis)
    first, last = (max(0, -steps), min(count, count - steps))
    return lax.ppermute(value, axis, [(source, source + steps) for source in range(first, last)])


def weights_of(region_ids, conductivity):
    table = jnp.arange(conductivity.shape[0], dtype=jnp.int32)
    picked = jnp.where(
        region_ids[:, :, None] == table[None, None, :],
        conductivity[None, None, :],
        jnp.zeros((), conductivity.dtype),
    )
    return jnp.sum(picked, axis=-1) / 36.0


def element_terms(field, below, weight):
    lower = jnp.concatenate([field, below[None]], 0)
    padded = jnp.pad(lower, ((0, 0), (0, 1), (0, 0)))
    corner_a = padded[:-1, :-1]
    corner_b = padded[:-1, 1:]
    corner_e = padded[1:, :-1]
    corner_d = padded[1:, 1:]
    scaled = weight[:, :, None]
    to_a = scaled * (4.0 * corner_a + 2.0 * corner_b + 2.0 * corner_e + corner_d)
    to_b = scaled * (2.0 * corner_a + 4.0 * corner_b + corner_e + 2.0 * corner_d)
    to_e = scaled * (2.0 * corner_a + corner_b + 4.0 * corner_e + 2.0 * corner_d)
    to_d = scaled * (corner_a + 2.0 * corner_b + 2.0 * corner_e + 4.0 * corner_d)
    total = jnp.pad(to_a, ((0, 1), (0, 1), (0, 0))) + jnp.pad(to_b, ((0, 1), (1, 0), (0, 0)))
    total = (
        total + jnp.pad(to_e, ((1, 0), (0, 1), (0, 0))) + jnp.pad(to_d, ((1, 0), (1, 0), (0, 0)))
    )
    return total


def contract(left, right):
    return lax.dot_general(
        left,
        right,
        (((0,), (0,)), ((), ())),
        precision=lax.Precision.HIGH,
        preferred_element_type=jnp.float32,
    )


def pairs(count, to):
    return [(i, to(i)) for i in range(count)]


def square_gather(block, axis):
    count, half = lax.axis_size(axis), block.shape[0] // 2
    to_x, to_z = pairs(count, lambda i: i ^ 1), pairs(count, lambda i: i ^ 2)
    x_low = lax.ppermute(block[:half], axis, to_x)
    z_high = lax.ppermute(block[half:], axis, to_z)
    x_high = lax.ppermute(block[half:], axis, to_x)
    z_low = lax.ppermute(block[:half], axis, to_z)
    corner = [lax.ppermute(x_low, axis, to_z), lax.ppermute(z_high, axis, to_x)]
    return [block, [x_low, x_high], [z_low, z_high], corner]


def ring_gather(block, axis):
    count, half = lax.axis_size(axis), block.shape[0] // 2
    up = pairs(count, lambda i: (i + 1) % count)
    down = pairs(count, lambda i: (i - 1) % count)
    left_low = lax.ppermute(block[:half], axis, up)
    right_high = lax.ppermute(block[half:], axis, down)
    left_high = lax.ppermute(block[half:], axis, up)
    right_low = lax.ppermute(block[:half], axis, down)
    far = [lax.ppermute(left_low, axis, up), lax.ppermute(right_high, axis, down)]
    return [block, [left_low, left_high], far, [right_low, right_high]]


def joined(block):
    return jnp.concatenate(block, 0) if isinstance(block, list) else block


def two_bit_xor(a, b):
    both = (a % 2) * (b % 2) + 2 * ((a // 2) * (b // 2))
    return a + b - 2 * both


def owners_kernel(side, tiles, part_ref, out_ref, slots, send_sems, recv_sems):
    me_r, me_c, me_t = lax.axis_index("r"), lax.axis_index("c"), lax.axis_index("mesh")
    halves = tiles // 2
    parity = me_t % 2
    sends = []
    for i in range(halves):
        j = 2 * i + parity
        dest_c = j // side
        dest_t = me_c + side * (j % side)
        to_self = jnp.logical_and(dest_c == me_c, dest_t == me_t)
        copy = pltpu.make_async_remote_copy(
            src_ref=part_ref.at[i],
            dst_ref=slots.at[me_t // 2],
            send_sem=send_sems.at[i],
            recv_sem=recv_sems.at[me_t // 2],
            device_id=(me_r, dest_c, dest_t),
            device_id_type=pl.DeviceIdType.MESH,
        )
        sends.append((copy, to_self, i))

        @pl.when(jnp.logical_not(to_self))
        def _():
            copy.start()

    for copy, to_self, i in sends:

        @pl.when(to_self)
        def _():
            slots[me_t // 2] = part_ref[i]

    incoming = (me_t // side) % 2
    mine = jnp.logical_and(me_t % side == me_c, parity == incoming)
    for source in range(halves):
        arrival = pltpu.make_async_remote_copy(
            src_ref=slots.at[source],
            dst_ref=slots.at[source],
            send_sem=send_sems.at[source],
            recv_sem=recv_sems.at[source],
            device_id=(me_r, me_c, me_t),
            device_id_type=pl.DeviceIdType.MESH,
        )

        @pl.when(jnp.logical_not(jnp.logical_and(mine, me_t // 2 == source)))
        def _():
            arrival.wait_recv()

    for copy, to_self, _ in sends:

        @pl.when(jnp.logical_not(to_self))
        def _():
            copy.wait_send()

    acc = slots[0]
    for source in range(1, halves):
        acc = acc + slots[source]
    out_ref[...] = acc


def scatter_to_owners(blocks, side, tiles):
    width = blocks.shape[-1]
    me_r, me_c, me_t = lax.axis_index("r"), lax.axis_index("c"), lax.axis_index("mesh")
    halves = tiles // 2
    index = jnp.arange(halves, dtype=jnp.int32)

    def pieces(parity):
        j = 2 * index + parity
        return blocks[two_bit_xor(me_c, j // side), (me_r - j % side) % side]

    parity = me_t % 2
    kept = pieces(parity) + lax.ppermute(pieces(1 - parity), "mesh", pairs(tiles, lambda i: i ^ 1))
    return pl.pallas_call(
        functools.partial(owners_kernel, side, tiles),
        out_shape=jax.ShapeDtypeStruct((width, width), jnp.float32),
        in_specs=[pl.BlockSpec(memory_space=pltpu.VMEM)],
        out_specs=pl.BlockSpec(memory_space=pltpu.VMEM),
        scratch_shapes=[
            pltpu.VMEM((halves, width, width), jnp.float32),
            pltpu.SemaphoreType.DMA((halves,)),
            pltpu.SemaphoreType.DMA((halves,)),
        ],
        compiler_params=pltpu.CompilerParams(has_side_effects=True),
    )(kept)


def local(snapshots, region_ids, conductivity):
    strip, width = region_ids.shape
    node_rows, group_cols = snapshots.shape
    side = lax.axis_size("c")
    tiles = lax.axis_size("mesh")
    field = snapshots.reshape(strip, width, group_cols)
    weight = weights_of(region_ids, conductivity)
    below = passed_along(field[0], "mesh", -1)
    total = element_terms(field, below, weight)
    carried = passed_along(total[strip, :width], "mesh", 1)
    inner = total[:strip, :width]
    panel = jnp.concatenate([inner[:1] + carried[None], inner[1:]], 0).reshape(
        node_rows, group_cols
    )
    rows = square_gather(panel, "c")
    cols = ring_gather(snapshots, "r")
    relayed_row, relayed_col = len(rows) - 1, len(cols) // 2

    def product(k1, k2):
        if k1 == relayed_row or k2 == relayed_col:
            half = node_rows // 2
            a, b = rows[k1], cols[k2]
            a = a if isinstance(a, list) else [a[:half], a[half:]]
            b = b if isinstance(b, list) else [b[:half], b[half:]]
            return contract(a[0], b[0]) + contract(a[1], b[1])
        return contract(joined(rows[k1]), joined(cols[k2]))

    blocks = jnp.stack(
        [jnp.stack([product(k1, k2) for k2 in range(side)], 0) for k1 in range(side)], 0
    )
    placed = scatter_to_owners(blocks, side, tiles)
    total_nodes = node_rows * tiles
    return placed / math.sqrt(total_nodes)


def solution(mesh):
    snap = mesh.shape["snap"]
    side = math.isqrt(snap)
    grid = Mesh(
        mesh.devices.reshape(snap // side, side, mesh.shape["mesh"]), ("r", "c", "mesh")
    )
    return jax.shard_map(
        local,
        mesh=grid,
        in_specs=(P("mesh", ("r", "c")), P("mesh", None), P()),
        out_specs=P(("r", "c"), "mesh"),
        check_vma=False,
    )
```

```python
import functools
import math

import jax
import jax.numpy as jnp
from jax import lax
from jax.experimental import pallas as pl
from jax.experimental.pallas import tpu as pltpu
from jax.sharding import Mesh
from jax.sharding import PartitionSpec as P


def passed_along(value, axis, steps):
    count = lax.axis_size(axis)
    first, last = (max(0, -steps), min(count, count - steps))
    return lax.ppermute(value, axis, [(source, source + steps) for source in range(first, last)])


def weights_of(region_ids, conductivity):
    table = jnp.arange(conductivity.shape[0], dtype=jnp.int32)
    picked = jnp.where(
        region_ids[:, :, None] == table[None, None, :],
        conductivity[None, None, :],
        jnp.zeros((), conductivity.dtype),
    )
    return jnp.sum(picked, axis=-1) / 36.0


def element_terms(field, below, weight):
    lower = jnp.concatenate([field, below[None]], 0)
    padded = jnp.pad(lower, ((0, 0), (0, 1), (0, 0)))
    corner_a = padded[:-1, :-1]
    corner_b = padded[:-1, 1:]
    corner_e = padded[1:, :-1]
    corner_d = padded[1:, 1:]
    scaled = weight[:, :, None]
    to_a = scaled * (4.0 * corner_a + 2.0 * corner_b + 2.0 * corner_e + corner_d)
    to_b = scaled * (2.0 * corner_a + 4.0 * corner_b + corner_e + 2.0 * corner_d)
    to_e = scaled * (2.0 * corner_a + corner_b + 4.0 * corner_e + 2.0 * corner_d)
    to_d = scaled * (corner_a + 2.0 * corner_b + 2.0 * corner_e + 4.0 * corner_d)
    total = jnp.pad(to_a, ((0, 1), (0, 1), (0, 0))) + jnp.pad(to_b, ((0, 1), (1, 0), (0, 0)))
    total = (
        total + jnp.pad(to_e, ((1, 0), (0, 1), (0, 0))) + jnp.pad(to_d, ((1, 0), (1, 0), (0, 0)))
    )
    return total


def contract(left, right):
    return lax.dot_general(
        left,
        right,
        (((0,), (0,)), ((), ())),
        precision=lax.Precision.HIGH,
        preferred_element_type=jnp.float32,
    )


def pairs(count, to):
    return [(i, to(i)) for i in range(count)]


def square_gather(block, axis):
    count, half = lax.axis_size(axis), block.shape[0] // 2
    to_x, to_z = pairs(count, lambda i: i ^ 1), pairs(count, lambda i: i ^ 2)
    x_low = lax.ppermute(block[:half], axis, to_x)
    z_high = lax.ppermute(block[half:], axis, to_z)
    x_high = lax.ppermute(block[half:], axis, to_x)
    z_low = lax.ppermute(block[:half], axis, to_z)
    corner = [lax.ppermute(x_low, axis, to_z), lax.ppermute(z_high, axis, to_x)]
    return [block, [x_low, x_high], [z_low, z_high], corner]


def ring_gather(block, axis):
    count, half = lax.axis_size(axis), block.shape[0] // 2
    up = pairs(count, lambda i: (i + 1) % count)
    down = pairs(count, lambda i: (i - 1) % count)
    left_low = lax.ppermute(block[:half], axis, up)
    right_high = lax.ppermute(block[half:], axis, down)
    left_high = lax.ppermute(block[half:], axis, up)
    right_low = lax.ppermute(block[:half], axis, down)
    far = [lax.ppermute(left_low, axis, up), lax.ppermute(right_high, axis, down)]
    return [block, [left_low, left_high], far, [right_low, right_high]]


def joined(block):
    return jnp.concatenate(block, 0) if isinstance(block, list) else block


def two_bit_xor(a, b):
    both = (a % 2) * (b % 2) + 2 * ((a // 2) * (b // 2))
    return a + b - 2 * both


def owners_kernel(side, tiles, part_ref, out_ref, slots, send_sems, recv_sems):
    me_r, me_c, me_t = lax.axis_index("r"), lax.axis_index("c"), lax.axis_index("mesh")
    halves = tiles // 2
    parity = me_t % 2
    incoming = (me_t // side) % 2

    def same(a, b):
        gap = a - b
        return 1 - (gap * gap + 15) // 16

    alone = same(me_t % side, me_c) * same(parity, incoming)
    barrier = pltpu.get_barrier_semaphore()
    for i in range(halves):
        j = 2 * i + parity

        @pl.when(jnp.logical_not(jnp.logical_and(j // side == me_c, me_c + side * (j % side) == me_t)))
        def _():
            pl.semaphore_signal(
                barrier, 1, device_id=(me_r, j // side, me_c + side * (j % side)),
                device_id_type=pl.DeviceIdType.MESH,
            )

    for source in range(halves):

        @pl.when(jnp.logical_not(jnp.logical_and(alone == 1, me_t // 2 == source)))
        def _():
            pl.semaphore_signal(
                barrier, 1, device_id=(me_r, me_t % side, 2 * source + incoming),
                device_id_type=pl.DeviceIdType.MESH,
            )

    pl.semaphore_wait(barrier, 2 * (halves - alone))
    sends = []
    for i in range(halves):
        j = 2 * i + parity
        dest_c = j // side
        dest_t = me_c + side * (j % side)
        to_self = jnp.logical_and(dest_c == me_c, dest_t == me_t)
        copy = pltpu.make_async_remote_copy(
            src_ref=part_ref.at[i],
            dst_ref=slots.at[me_t // 2],
            send_sem=send_sems.at[i],
            recv_sem=recv_sems.at[me_t // 2],
            device_id=(me_r, dest_c, dest_t),
            device_id_type=pl.DeviceIdType.MESH,
        )
        sends.append((copy, to_self, i))

        @pl.when(jnp.logical_not(to_self))
        def _():
            copy.start()

    for copy, to_self, i in sends:

        @pl.when(to_self)
        def _():
            slots[me_t // 2] = part_ref[i]

    mine = alone == 1
    for source in range(halves):
        arrival = pltpu.make_async_remote_copy(
            src_ref=slots.at[source],
            dst_ref=slots.at[source],
            send_sem=send_sems.at[source],
            recv_sem=recv_sems.at[source],
            device_id=(me_r, me_c, me_t),
            device_id_type=pl.DeviceIdType.MESH,
        )

        @pl.when(jnp.logical_not(jnp.logical_and(mine, me_t // 2 == source)))
        def _():
            arrival.wait_recv()

    for copy, to_self, _ in sends:

        @pl.when(jnp.logical_not(to_self))
        def _():
            copy.wait_send()

    acc = slots[0]
    for source in range(1, halves):
        acc = acc + slots[source]
    out_ref[...] = acc


def scatter_to_owners(blocks, side, tiles):
    width = blocks.shape[-1]
    me_r, me_c, me_t = lax.axis_index("r"), lax.axis_index("c"), lax.axis_index("mesh")
    halves = tiles // 2
    index = jnp.arange(halves, dtype=jnp.int32)

    def pieces(parity):
        j = 2 * index + parity
        return blocks[two_bit_xor(me_c, j // side), (me_r - j % side) % side]

    parity = me_t % 2
    kept = pieces(parity) + lax.ppermute(pieces(1 - parity), "mesh", pairs(tiles, lambda i: i ^ 1))
    return pl.pallas_call(
        functools.partial(owners_kernel, side, tiles),
        out_shape=jax.ShapeDtypeStruct((width, width), jnp.float32),
        in_specs=[pl.BlockSpec(memory_space=pltpu.VMEM)],
        out_specs=pl.BlockSpec(memory_space=pltpu.VMEM),
        scratch_shapes=[
            pltpu.VMEM((halves, width, width), jnp.float32),
            pltpu.SemaphoreType.DMA((halves,)),
            pltpu.SemaphoreType.DMA((halves,)),
        ],
        compiler_params=pltpu.CompilerParams(collective_id=0, has_side_effects=True),
    )(kept)


def local(snapshots, region_ids, conductivity):
    strip, width = region_ids.shape
    node_rows, group_cols = snapshots.shape
    side = lax.axis_size("c")
    tiles = lax.axis_size("mesh")
    field = snapshots.reshape(strip, width, group_cols)
    weight = weights_of(region_ids, conductivity)
    below = passed_along(field[0], "mesh", -1)
    total = element_terms(field, below, weight)
    carried = passed_along(total[strip, :width], "mesh", 1)
    inner = total[:strip, :width]
    panel = jnp.concatenate([inner[:1] + carried[None], inner[1:]], 0).reshape(
        node_rows, group_cols
    )
    rows = square_gather(panel, "c")
    cols = ring_gather(snapshots, "r")
    relayed_row, relayed_col = len(rows) - 1, len(cols) // 2

    def product(k1, k2):
        if k1 == relayed_row or k2 == relayed_col:
            half = node_rows // 2
            a, b = rows[k1], cols[k2]
            a = a if isinstance(a, list) else [a[:half], a[half:]]
            b = b if isinstance(b, list) else [b[:half], b[half:]]
            return contract(a[0], b[0]) + contract(a[1], b[1])
        return contract(joined(rows[k1]), joined(cols[k2]))

    blocks = jnp.stack(
        [jnp.stack([product(k1, k2) for k2 in range(side)], 0) for k1 in range(side)], 0
    )
    placed = scatter_to_owners(blocks, side, tiles)
    total_nodes = node_rows * tiles
    return placed / math.sqrt(total_nodes)


def solution(mesh):
    snap = mesh.shape["snap"]
    side = math.isqrt(snap)
    grid = Mesh(
        mesh.devices.reshape(snap // side, side, mesh.shape["mesh"]), ("r", "c", "mesh")
    )
    return jax.shard_map(
        local,
        mesh=grid,
        in_specs=(P("mesh", ("r", "c")), P("mesh", None), P()),
        out_specs=P(("r", "c"), "mesh"),
        check_vma=False,
    )
```

```python
import functools
import math

import jax
import jax.numpy as jnp
from jax import lax
from jax.experimental import pallas as pl
from jax.experimental.pallas import tpu as pltpu
from jax.sharding import Mesh
from jax.sharding import PartitionSpec as P


def passed_along(value, axis, steps):
    count = lax.axis_size(axis)
    first, last = (max(0, -steps), min(count, count - steps))
    return lax.ppermute(value, axis, [(source, source + steps) for source in range(first, last)])


def weights_of(region_ids, conductivity):
    table = jnp.arange(conductivity.shape[0], dtype=jnp.int32)
    picked = jnp.where(
        region_ids[:, :, None] == table[None, None, :],
        conductivity[None, None, :],
        jnp.zeros((), conductivity.dtype),
    )
    return jnp.sum(picked, axis=-1) / 36.0


def element_terms(field, below, weight):
    lower = jnp.concatenate([field, below[None]], 0)
    padded = jnp.pad(lower, ((0, 0), (0, 1), (0, 0)))
    corner_a = padded[:-1, :-1]
    corner_b = padded[:-1, 1:]
    corner_e = padded[1:, :-1]
    corner_d = padded[1:, 1:]
    scaled = weight[:, :, None]
    to_a = scaled * (4.0 * corner_a + 2.0 * corner_b + 2.0 * corner_e + corner_d)
    to_b = scaled * (2.0 * corner_a + 4.0 * corner_b + corner_e + 2.0 * corner_d)
    to_e = scaled * (2.0 * corner_a + corner_b + 4.0 * corner_e + 2.0 * corner_d)
    to_d = scaled * (corner_a + 2.0 * corner_b + 2.0 * corner_e + 4.0 * corner_d)
    total = jnp.pad(to_a, ((0, 1), (0, 1), (0, 0))) + jnp.pad(to_b, ((0, 1), (1, 0), (0, 0)))
    total = (
        total + jnp.pad(to_e, ((1, 0), (0, 1), (0, 0))) + jnp.pad(to_d, ((1, 0), (1, 0), (0, 0)))
    )
    return total


def contract(left, right):
    return lax.dot_general(
        left,
        right,
        (((0,), (0,)), ((), ())),
        precision=lax.Precision.HIGH,
        preferred_element_type=jnp.float32,
    )


def pairs(count, to):
    return [(i, to(i)) for i in range(count)]


def square_gather(block, axis):
    count, half = lax.axis_size(axis), block.shape[0] // 2
    to_x, to_z = pairs(count, lambda i: i ^ 1), pairs(count, lambda i: i ^ 2)
    x_low = lax.ppermute(block[:half], axis, to_x)
    z_high = lax.ppermute(block[half:], axis, to_z)
    x_high = lax.ppermute(block[half:], axis, to_x)
    z_low = lax.ppermute(block[:half], axis, to_z)
    corner = [lax.ppermute(x_low, axis, to_z), lax.ppermute(z_high, axis, to_x)]
    return [block, [x_low, x_high], [z_low, z_high], corner]


def ring_gather(block, axis):
    count, half = lax.axis_size(axis), block.shape[0] // 2
    up = pairs(count, lambda i: (i + 1) % count)
    down = pairs(count, lambda i: (i - 1) % count)
    left_low = lax.ppermute(block[:half], axis, up)
    right_high = lax.ppermute(block[half:], axis, down)
    left_high = lax.ppermute(block[half:], axis, up)
    right_low = lax.ppermute(block[:half], axis, down)
    far = [lax.ppermute(left_low, axis, up), lax.ppermute(right_high, axis, down)]
    return [block, [left_low, left_high], far, [right_low, right_high]]


def joined(block):
    return jnp.concatenate(block, 0) if isinstance(block, list) else block


def two_bit_xor(a, b):
    both = (a % 2) * (b % 2) + 2 * ((a // 2) * (b // 2))
    return a + b - 2 * both


def owners_kernel(side, tiles, part_ref, out_ref, slots, send_sems, recv_sems):
    me_r, me_c, me_t = lax.axis_index("r"), lax.axis_index("c"), lax.axis_index("mesh")
    halves = tiles // 2
    parity = me_t % 2
    incoming = (me_t // side) % 2

    def same(a, b):
        gap = a - b
        return 1 - (gap * gap + 15) // 16

    alone = same(me_t % side, me_c) * same(parity, incoming)
    barrier = pltpu.get_barrier_semaphore()
    for i in range(halves):
        j = 2 * i + parity

        @pl.when(jnp.logical_not(jnp.logical_and(j // side == me_c, me_c + side * (j % side) == me_t)))
        def _():
            pl.semaphore_signal(
                barrier, 1, device_id=(me_r, j // side, me_c + side * (j % side)),
                device_id_type=pl.DeviceIdType.MESH,
            )

    for source in range(halves):

        @pl.when(jnp.logical_not(jnp.logical_and(alone == 1, me_t // 2 == source)))
        def _():
            pl.semaphore_signal(
                barrier, 1, device_id=(me_r, me_t % side, 2 * source + incoming),
                device_id_type=pl.DeviceIdType.MESH,
            )

    pl.semaphore_wait(barrier, 2 * (halves - alone))
    sends = []
    for i in range(halves):
        j = 2 * i + parity
        dest_c = j // side
        dest_t = me_c + side * (j % side)
        to_self = jnp.logical_and(dest_c == me_c, dest_t == me_t)
        copy = pltpu.make_async_remote_copy(
            src_ref=part_ref.at[i],
            dst_ref=slots.at[me_t // 2],
            send_sem=send_sems.at[i],
            recv_sem=recv_sems.at[me_t // 2],
            device_id=(me_r, dest_c, dest_t),
            device_id_type=pl.DeviceIdType.MESH,
        )
        sends.append((copy, to_self, i))

        @pl.when(jnp.logical_not(to_self))
        def _():
            copy.start()

    for copy, to_self, i in sends:

        @pl.when(to_self)
        def _():
            slots[me_t // 2] = part_ref[i]

    mine = alone == 1
    for source in range(halves):
        arrival = pltpu.make_async_remote_copy(
            src_ref=slots.at[source],
            dst_ref=slots.at[source],
            send_sem=send_sems.at[source],
            recv_sem=recv_sems.at[source],
            device_id=(me_r, me_c, me_t),
            device_id_type=pl.DeviceIdType.MESH,
        )

        @pl.when(jnp.logical_not(jnp.logical_and(mine, me_t // 2 == source)))
        def _():
            arrival.wait_recv()

    for copy, to_self, _ in sends:

        @pl.when(jnp.logical_not(to_self))
        def _():
            copy.wait_send()

    acc = slots[0]
    for source in range(1, halves):
        acc = acc + slots[source]
    out_ref[...] = acc


def scatter_to_owners(blocks, side, tiles, scale):
    width = blocks.shape[-1]
    me_r, me_c, me_t = lax.axis_index("r"), lax.axis_index("c"), lax.axis_index("mesh")
    halves = tiles // 2
    index = jnp.arange(halves, dtype=jnp.int32)

    def pieces(parity):
        j = 2 * index + parity
        return blocks[two_bit_xor(me_c, j // side), (me_r - j % side) % side]

    parity = me_t % 2
    kept = (pieces(parity) + lax.ppermute(pieces(1 - parity), "mesh", pairs(tiles, lambda i: i ^ 1))) / scale
    return pl.pallas_call(
        functools.partial(owners_kernel, side, tiles),
        out_shape=jax.ShapeDtypeStruct((width, width), jnp.float32),
        in_specs=[pl.BlockSpec(memory_space=pltpu.VMEM)],
        out_specs=pl.BlockSpec(memory_space=pltpu.VMEM),
        scratch_shapes=[
            pltpu.VMEM((halves, width, width), jnp.float32),
            pltpu.SemaphoreType.DMA((halves,)),
            pltpu.SemaphoreType.DMA((halves,)),
        ],
        compiler_params=pltpu.CompilerParams(collective_id=0, has_side_effects=True),
    )(kept)


def local(snapshots, region_ids, conductivity):
    strip, width = region_ids.shape
    node_rows, group_cols = snapshots.shape
    side = lax.axis_size("c")
    tiles = lax.axis_size("mesh")
    field = snapshots.reshape(strip, width, group_cols)
    weight = weights_of(region_ids, conductivity)
    below = passed_along(field[0], "mesh", -1)
    total = element_terms(field, below, weight)
    carried = passed_along(total[strip, :width], "mesh", 1)
    inner = total[:strip, :width]
    panel = jnp.concatenate([inner[:1] + carried[None], inner[1:]], 0).reshape(
        node_rows, group_cols
    )
    rows = square_gather(panel, "c")
    cols = ring_gather(snapshots, "r")
    relayed_row, relayed_col = len(rows) - 1, len(cols) // 2

    def product(k1, k2):
        if k1 == relayed_row or k2 == relayed_col:
            half = node_rows // 2
            a, b = rows[k1], cols[k2]
            a = a if isinstance(a, list) else [a[:half], a[half:]]
            b = b if isinstance(b, list) else [b[:half], b[half:]]
            return contract(a[0], b[0]) + contract(a[1], b[1])
        return contract(joined(rows[k1]), joined(cols[k2]))

    blocks = jnp.stack(
        [jnp.stack([product(k1, k2) for k2 in range(side)], 0) for k1 in range(side)], 0
    )
    return scatter_to_owners(blocks, side, tiles, math.sqrt(node_rows * tiles))


def solution(mesh):
    snap = mesh.shape["snap"]
    side = math.isqrt(snap)
    grid = Mesh(
        mesh.devices.reshape(snap // side, side, mesh.shape["mesh"]), ("r", "c", "mesh")
    )
    return jax.shard_map(
        local,
        mesh=grid,
        in_specs=(P("mesh", ("r", "c")), P("mesh", None), P()),
        out_specs=P(("r", "c"), "mesh"),
        check_vma=False,
    )
```

```python
import functools
import math

import jax
import jax.numpy as jnp
from jax import lax
from jax.experimental import pallas as pl
from jax.experimental.pallas import tpu as pltpu
from jax.sharding import Mesh
from jax.sharding import PartitionSpec as P


def passed_along(value, axis, steps):
    count = lax.axis_size(axis)
    first, last = (max(0, -steps), min(count, count - steps))
    return lax.ppermute(value, axis, [(source, source + steps) for source in range(first, last)])


def weights_of(region_ids, conductivity):
    table = jnp.arange(conductivity.shape[0], dtype=jnp.int32)
    picked = jnp.where(
        region_ids[:, :, None] == table[None, None, :],
        conductivity[None, None, :],
        jnp.zeros((), conductivity.dtype),
    )
    return jnp.sum(picked, axis=-1) / 36.0


def element_terms(field, below, weight):
    lower = jnp.concatenate([field, below[None]], 0)
    padded = jnp.pad(lower, ((0, 0), (0, 1), (0, 0)))
    corner_a = padded[:-1, :-1]
    corner_b = padded[:-1, 1:]
    corner_e = padded[1:, :-1]
    corner_d = padded[1:, 1:]
    scaled = weight[:, :, None]
    to_a = scaled * (4.0 * corner_a + 2.0 * corner_b + 2.0 * corner_e + corner_d)
    to_b = scaled * (2.0 * corner_a + 4.0 * corner_b + corner_e + 2.0 * corner_d)
    to_e = scaled * (2.0 * corner_a + corner_b + 4.0 * corner_e + 2.0 * corner_d)
    to_d = scaled * (corner_a + 2.0 * corner_b + 2.0 * corner_e + 4.0 * corner_d)
    total = jnp.pad(to_a, ((0, 1), (0, 1), (0, 0))) + jnp.pad(to_b, ((0, 1), (1, 0), (0, 0)))
    total = (
        total + jnp.pad(to_e, ((1, 0), (0, 1), (0, 0))) + jnp.pad(to_d, ((1, 0), (1, 0), (0, 0)))
    )
    return total


def contract(left, right):
    return lax.dot_general(
        left,
        right,
        (((0,), (0,)), ((), ())),
        precision=lax.Precision.HIGH,
        preferred_element_type=jnp.float32,
    )


def pairs(count, to):
    return [(i, to(i)) for i in range(count)]


def square_gather(block, axis):
    count, half = lax.axis_size(axis), block.shape[0] // 2
    to_x, to_z = pairs(count, lambda i: i ^ 1), pairs(count, lambda i: i ^ 2)
    x_low = lax.ppermute(block[:half], axis, to_x)
    z_high = lax.ppermute(block[half:], axis, to_z)
    x_high = lax.ppermute(block[half:], axis, to_x)
    z_low = lax.ppermute(block[:half], axis, to_z)
    corner = [lax.ppermute(x_low, axis, to_z), lax.ppermute(z_high, axis, to_x)]
    return [block, [x_low, x_high], [z_low, z_high], corner]


def ring_gather(block, axis):
    count, half = lax.axis_size(axis), block.shape[0] // 2
    up = pairs(count, lambda i: (i + 1) % count)
    down = pairs(count, lambda i: (i - 1) % count)
    left_low = lax.ppermute(block[:half], axis, up)
    right_high = lax.ppermute(block[half:], axis, down)
    left_high = lax.ppermute(block[half:], axis, up)
    right_low = lax.ppermute(block[:half], axis, down)
    far = [lax.ppermute(left_low, axis, up), lax.ppermute(right_high, axis, down)]
    return [block, [left_low, left_high], far, [right_low, right_high]]


def joined(block):
    return jnp.concatenate(block, 0) if isinstance(block, list) else block


def two_bit_xor(a, b):
    both = (a % 2) * (b % 2) + 2 * ((a // 2) * (b // 2))
    return a + b - 2 * both


def owners_kernel(side, tiles, part_ref, out_ref, slots, send_sems, recv_sems):
    me_r, me_c, me_t = lax.axis_index("r"), lax.axis_index("c"), lax.axis_index("mesh")
    halves = tiles // 2
    parity = me_t % 2
    incoming = (me_t // side) % 2

    def same(a, b):
        gap = a - b
        return 1 - (gap * gap + 15) // 16

    alone = same(me_t % side, me_c) * same(parity, incoming)
    barrier = pltpu.get_barrier_semaphore()
    for i in range(halves):
        j = 2 * i + parity

        @pl.when(jnp.logical_not(jnp.logical_and(j // side == me_c, me_c + side * (j % side) == me_t)))
        def _():
            pl.semaphore_signal(
                barrier, 1, device_id=(me_r, j // side, me_c + side * (j % side)),
                device_id_type=pl.DeviceIdType.MESH,
            )

    for source in range(halves):

        @pl.when(jnp.logical_not(jnp.logical_and(alone == 1, me_t // 2 == source)))
        def _():
            pl.semaphore_signal(
                barrier, 1, device_id=(me_r, me_t % side, 2 * source + incoming),
                device_id_type=pl.DeviceIdType.MESH,
            )

    pl.semaphore_wait(barrier, 2 * (halves - alone))
    sends = []
    for i in range(halves):
        j = 2 * i + parity
        dest_c = j // side
        dest_t = me_c + side * (j % side)
        to_self = jnp.logical_and(dest_c == me_c, dest_t == me_t)
        copy = pltpu.make_async_remote_copy(
            src_ref=part_ref.at[i],
            dst_ref=slots.at[me_t // 2],
            send_sem=send_sems.at[i],
            recv_sem=recv_sems.at[me_t // 2],
            device_id=(me_r, dest_c, dest_t),
            device_id_type=pl.DeviceIdType.MESH,
        )
        sends.append((copy, to_self, i))

        @pl.when(jnp.logical_not(to_self))
        def _():
            copy.start()

    for copy, to_self, i in sends:

        @pl.when(to_self)
        def _():
            slots[me_t // 2] = part_ref[i]

    mine = alone == 1
    for source in range(halves):
        arrival = pltpu.make_async_remote_copy(
            src_ref=slots.at[source],
            dst_ref=slots.at[source],
            send_sem=send_sems.at[source],
            recv_sem=recv_sems.at[source],
            device_id=(me_r, me_c, me_t),
            device_id_type=pl.DeviceIdType.MESH,
        )

        @pl.when(jnp.logical_not(jnp.logical_and(mine, me_t // 2 == source)))
        def _():
            arrival.wait_recv()

    for copy, to_self, _ in sends:

        @pl.when(jnp.logical_not(to_self))
        def _():
            copy.wait_send()

    acc = slots[0]
    for source in range(1, halves):
        acc = acc + slots[source]
    out_ref[...] = acc


def scatter_to_owners(blocks, side, tiles, scale):
    width = blocks.shape[-1]
    me_r, me_c, me_t = lax.axis_index("r"), lax.axis_index("c"), lax.axis_index("mesh")
    halves = tiles // 2
    index = jnp.arange(halves, dtype=jnp.int32)

    def pieces(parity):
        j = 2 * index + parity
        return blocks[two_bit_xor(me_c, j // side), (me_r - j % side) % side]

    parity = me_t % 2
    kept = (pieces(parity) + lax.ppermute(pieces(1 - parity), "mesh", pairs(tiles, lambda i: i ^ 1))) / scale
    return pl.pallas_call(
        functools.partial(owners_kernel, side, tiles),
        out_shape=jax.ShapeDtypeStruct((width, width), jnp.float32),
        in_specs=[pl.BlockSpec(memory_space=pltpu.VMEM)],
        out_specs=pl.BlockSpec(memory_space=pltpu.VMEM),
        scratch_shapes=[
            pltpu.VMEM((halves, width, width), jnp.float32),
            pltpu.SemaphoreType.DMA((halves,)),
            pltpu.SemaphoreType.DMA((halves,)),
        ],
        compiler_params=pltpu.CompilerParams(collective_id=0, has_side_effects=True),
    )(kept)


def local(snapshots, region_ids, conductivity):
    strip, width = region_ids.shape
    node_rows, group_cols = snapshots.shape
    side = lax.axis_size("c")
    tiles = lax.axis_size("mesh")
    field = snapshots.reshape(strip, width, group_cols)
    weight = weights_of(region_ids, conductivity)
    below = passed_along(field[0], "mesh", -1)
    total = element_terms(field, below, weight)
    carried = passed_along(total[strip, :width], "mesh", 1)
    inner = total[:strip, :width]
    panel = jnp.concatenate([inner[:1] + carried[None], inner[1:]], 0).reshape(
        node_rows, group_cols
    )
    rows = square_gather(panel, "c")
    cols = ring_gather(snapshots, "r")
    relayed_row, relayed_col = len(rows) - 1, len(cols) // 2
    half = node_rows // 2

    def halves_of(block):
        return block if isinstance(block, list) else [block[:half], block[half:]]

    row_halves = [halves_of(a) for a in rows]
    col_halves = [halves_of(b) for b in cols]
    plain_cols = [k2 for k2 in range(side) if k2 != relayed_col]
    far = sum(
        contract(jnp.concatenate([r[p] for r in row_halves], 1), col_halves[relayed_col][p])
        for p in range(2)
    )
    corner = sum(
        contract(row_halves[relayed_row][p], jnp.concatenate([col_halves[k][p] for k in plain_cols], 1))
        for p in range(2)
    )

    def product(k1, k2):
        if k2 == relayed_col:
            return far[k1 * group_cols : (k1 + 1) * group_cols]
        if k1 == relayed_row:
            at = plain_cols.index(k2) * group_cols
            return corner[:, at : at + group_cols]
        return contract(joined(rows[k1]), joined(cols[k2]))

    blocks = jnp.stack(
        [jnp.stack([product(k1, k2) for k2 in range(side)], 0) for k1 in range(side)], 0
    )
    return scatter_to_owners(blocks, side, tiles, math.sqrt(node_rows * tiles))


def solution(mesh):
    snap = mesh.shape["snap"]
    side = math.isqrt(snap)
    grid = Mesh(
        mesh.devices.reshape(snap // side, side, mesh.shape["mesh"]), ("r", "c", "mesh")
    )
    return jax.shard_map(
        local,
        mesh=grid,
        in_specs=(P("mesh", ("r", "c")), P("mesh", None), P()),
        out_specs=P(("r", "c"), "mesh"),
        check_vma=False,
    )
```

```python
import functools
import math

import jax
import jax.numpy as jnp
from jax import lax
from jax.experimental import pallas as pl
from jax.experimental.pallas import tpu as pltpu
from jax.sharding import Mesh
from jax.sharding import PartitionSpec as P


def passed_along(value, axis, steps):
    count = lax.axis_size(axis)
    first, last = (max(0, -steps), min(count, count - steps))
    return lax.ppermute(value, axis, [(source, source + steps) for source in range(first, last)])


def weights_of(region_ids, conductivity):
    table = jnp.arange(conductivity.shape[0], dtype=jnp.int32)
    picked = jnp.where(
        region_ids[:, :, None] == table[None, None, :],
        conductivity[None, None, :],
        jnp.zeros((), conductivity.dtype),
    )
    return jnp.sum(picked, axis=-1) / 36.0


def element_terms(field, below, weight):
    lower = jnp.concatenate([field, below[None]], 0)
    padded = jnp.pad(lower, ((0, 0), (0, 1), (0, 0)))
    corner_a = padded[:-1, :-1]
    corner_b = padded[:-1, 1:]
    corner_e = padded[1:, :-1]
    corner_d = padded[1:, 1:]
    scaled = weight[:, :, None]
    to_a = scaled * (4.0 * corner_a + 2.0 * corner_b + 2.0 * corner_e + corner_d)
    to_b = scaled * (2.0 * corner_a + 4.0 * corner_b + corner_e + 2.0 * corner_d)
    to_e = scaled * (2.0 * corner_a + corner_b + 4.0 * corner_e + 2.0 * corner_d)
    to_d = scaled * (corner_a + 2.0 * corner_b + 2.0 * corner_e + 4.0 * corner_d)
    total = jnp.pad(to_a, ((0, 1), (0, 1), (0, 0))) + jnp.pad(to_b, ((0, 1), (1, 0), (0, 0)))
    total = (
        total + jnp.pad(to_e, ((1, 0), (0, 1), (0, 0))) + jnp.pad(to_d, ((1, 0), (1, 0), (0, 0)))
    )
    return total


def contract(left, right):
    return lax.dot_general(
        left,
        right,
        (((0,), (0,)), ((), ())),
        precision=lax.Precision.HIGH,
        preferred_element_type=jnp.float32,
    )


def pairs(count, to):
    return [(i, to(i)) for i in range(count)]


def square_gather(block, axis):
    count, half = lax.axis_size(axis), block.shape[0] // 2
    to_x, to_z = pairs(count, lambda i: i ^ 1), pairs(count, lambda i: i ^ 2)
    x_low = lax.ppermute(block[:half], axis, to_x)
    z_high = lax.ppermute(block[half:], axis, to_z)
    x_high = lax.ppermute(block[half:], axis, to_x)
    z_low = lax.ppermute(block[:half], axis, to_z)
    corner = [lax.ppermute(x_low, axis, to_z), lax.ppermute(z_high, axis, to_x)]
    return [block, [x_low, x_high], [z_low, z_high], corner]


def ring_gather(block, axis):
    count, half = lax.axis_size(axis), block.shape[0] // 2
    up = pairs(count, lambda i: (i + 1) % count)
    down = pairs(count, lambda i: (i - 1) % count)
    left_low = lax.ppermute(block[:half], axis, up)
    right_high = lax.ppermute(block[half:], axis, down)
    left_high = lax.ppermute(block[half:], axis, up)
    right_low = lax.ppermute(block[:half], axis, down)
    far = [lax.ppermute(left_low, axis, up), lax.ppermute(right_high, axis, down)]
    return [block, [left_low, left_high], far, [right_low, right_high]]


def joined(block):
    return jnp.concatenate(block, 0) if isinstance(block, list) else block


def two_bit_xor(a, b):
    both = (a % 2) * (b % 2) + 2 * ((a // 2) * (b // 2))
    return a + b - 2 * both


def owners_kernel(side, tiles, part_ref, slots, send_sems, recv_sems):
    me_r, me_c, me_t = lax.axis_index("r"), lax.axis_index("c"), lax.axis_index("mesh")
    halves = tiles // 2
    parity = me_t % 2
    incoming = (me_t // side) % 2

    def same(a, b):
        gap = a - b
        return 1 - (gap * gap + 15) // 16

    alone = same(me_t % side, me_c) * same(parity, incoming)
    barrier = pltpu.get_barrier_semaphore()
    for i in range(halves):
        j = 2 * i + parity

        @pl.when(jnp.logical_not(jnp.logical_and(j // side == me_c, me_c + side * (j % side) == me_t)))
        def _():
            pl.semaphore_signal(
                barrier, 1, device_id=(me_r, j // side, me_c + side * (j % side)),
                device_id_type=pl.DeviceIdType.MESH,
            )

    for source in range(halves):

        @pl.when(jnp.logical_not(jnp.logical_and(alone == 1, me_t // 2 == source)))
        def _():
            pl.semaphore_signal(
                barrier, 1, device_id=(me_r, me_t % side, 2 * source + incoming),
                device_id_type=pl.DeviceIdType.MESH,
            )

    pl.semaphore_wait(barrier, 2 * (halves - alone))
    sends = []
    for i in range(halves):
        j = 2 * i + parity
        dest_c = j // side
        dest_t = me_c + side * (j % side)
        to_self = jnp.logical_and(dest_c == me_c, dest_t == me_t)
        copy = pltpu.make_async_remote_copy(
            src_ref=part_ref.at[i],
            dst_ref=slots.at[me_t // 2],
            send_sem=send_sems.at[i],
            recv_sem=recv_sems.at[me_t // 2],
            device_id=(me_r, dest_c, dest_t),
            device_id_type=pl.DeviceIdType.MESH,
        )
        sends.append((copy, to_self, i))

        @pl.when(jnp.logical_not(to_self))
        def _():
            copy.start()

    for copy, to_self, i in sends:

        @pl.when(to_self)
        def _():
            slots[me_t // 2] = part_ref[i]

    mine = alone == 1
    for source in range(halves):
        arrival = pltpu.make_async_remote_copy(
            src_ref=slots.at[source],
            dst_ref=slots.at[source],
            send_sem=send_sems.at[source],
            recv_sem=recv_sems.at[source],
            device_id=(me_r, me_c, me_t),
            device_id_type=pl.DeviceIdType.MESH,
        )

        @pl.when(jnp.logical_not(jnp.logical_and(mine, me_t // 2 == source)))
        def _():
            arrival.wait_recv()

    for copy, to_self, _ in sends:

        @pl.when(jnp.logical_not(to_self))
        def _():
            copy.wait_send()


def scatter_to_owners(blocks, side, tiles, scale):
    width = blocks.shape[-1]
    me_r, me_c, me_t = lax.axis_index("r"), lax.axis_index("c"), lax.axis_index("mesh")
    halves = tiles // 2
    index = jnp.arange(halves, dtype=jnp.int32)

    def pieces(parity):
        j = 2 * index + parity
        return blocks[two_bit_xor(me_c, j // side), (me_r - j % side) % side]

    parity = me_t % 2
    kept = (pieces(parity) + lax.ppermute(pieces(1 - parity), "mesh", pairs(tiles, lambda i: i ^ 1))) / scale
    slots = pl.pallas_call(
        functools.partial(owners_kernel, side, tiles),
        out_shape=jax.ShapeDtypeStruct((halves, width, width), jnp.float32),
        in_specs=[pl.BlockSpec(memory_space=pltpu.VMEM)],
        out_specs=pl.BlockSpec(memory_space=pltpu.VMEM),
        scratch_shapes=[
            pltpu.SemaphoreType.DMA((halves,)),
            pltpu.SemaphoreType.DMA((halves,)),
        ],
        compiler_params=pltpu.CompilerParams(collective_id=0, has_side_effects=True),
    )(kept)
    return jnp.sum(slots, axis=0)


def local(snapshots, region_ids, conductivity):
    strip, width = region_ids.shape
    node_rows, group_cols = snapshots.shape
    side = lax.axis_size("c")
    tiles = lax.axis_size("mesh")
    field = snapshots.reshape(strip, width, group_cols)
    weight = weights_of(region_ids, conductivity)
    below = passed_along(field[0], "mesh", -1)
    total = element_terms(field, below, weight)
    carried = passed_along(total[strip, :width], "mesh", 1)
    inner = total[:strip, :width]
    panel = jnp.concatenate([inner[:1] + carried[None], inner[1:]], 0).reshape(
        node_rows, group_cols
    )
    rows = square_gather(panel, "c")
    cols = ring_gather(snapshots, "r")
    relayed_row, relayed_col = len(rows) - 1, len(cols) // 2

    def product(k1, k2):
        if k1 == relayed_row or k2 == relayed_col:
            half = node_rows // 2
            a, b = rows[k1], cols[k2]
            a = a if isinstance(a, list) else [a[:half], a[half:]]
            b = b if isinstance(b, list) else [b[:half], b[half:]]
            return contract(a[0], b[0]) + contract(a[1], b[1])
        return contract(joined(rows[k1]), joined(cols[k2]))

    blocks = jnp.stack(
        [jnp.stack([product(k1, k2) for k2 in range(side)], 0) for k1 in range(side)], 0
    )
    return scatter_to_owners(blocks, side, tiles, math.sqrt(node_rows * tiles))


def solution(mesh):
    snap = mesh.shape["snap"]
    side = math.isqrt(snap)
    grid = Mesh(
        mesh.devices.reshape(snap // side, side, mesh.shape["mesh"]), ("r", "c", "mesh")
    )
    return jax.shard_map(
        local,
        mesh=grid,
        in_specs=(P("mesh", ("r", "c")), P("mesh", None), P()),
        out_specs=P(("r", "c"), "mesh"),
        check_vma=False,
    )
```

```python
import functools
import math

import jax
import jax.numpy as jnp
from jax import lax
from jax.experimental import pallas as pl
from jax.experimental.pallas import tpu as pltpu
from jax.sharding import Mesh
from jax.sharding import PartitionSpec as P


def passed_along(value, axis, steps):
    count = lax.axis_size(axis)
    first, last = (max(0, -steps), min(count, count - steps))
    return lax.ppermute(value, axis, [(source, source + steps) for source in range(first, last)])


def weights_of(region_ids, conductivity):
    table = jnp.arange(conductivity.shape[0], dtype=jnp.int32)
    picked = jnp.where(
        region_ids[:, :, None] == table[None, None, :],
        conductivity[None, None, :],
        jnp.zeros((), conductivity.dtype),
    )
    return jnp.sum(picked, axis=-1) / 36.0


def element_terms(field, below, weight):
    lower = jnp.concatenate([field, below[None]], 0)
    padded = jnp.pad(lower, ((0, 0), (0, 1), (0, 0)))
    corner_a = padded[:-1, :-1]
    corner_b = padded[:-1, 1:]
    corner_e = padded[1:, :-1]
    corner_d = padded[1:, 1:]
    scaled = weight[:, :, None]
    to_a = scaled * (4.0 * corner_a + 2.0 * corner_b + 2.0 * corner_e + corner_d)
    to_b = scaled * (2.0 * corner_a + 4.0 * corner_b + corner_e + 2.0 * corner_d)
    to_e = scaled * (2.0 * corner_a + corner_b + 4.0 * corner_e + 2.0 * corner_d)
    to_d = scaled * (corner_a + 2.0 * corner_b + 2.0 * corner_e + 4.0 * corner_d)
    total = jnp.pad(to_a, ((0, 1), (0, 1), (0, 0))) + jnp.pad(to_b, ((0, 1), (1, 0), (0, 0)))
    total = (
        total + jnp.pad(to_e, ((1, 0), (0, 1), (0, 0))) + jnp.pad(to_d, ((1, 0), (1, 0), (0, 0)))
    )
    return total


def contract(left, right):
    return lax.dot_general(
        left,
        right,
        (((0,), (0,)), ((), ())),
        precision=lax.Precision.HIGH,
        preferred_element_type=jnp.float32,
    )


def pairs(count, to):
    return [(i, to(i)) for i in range(count)]


def square_gather(block, axis):
    count, half = lax.axis_size(axis), block.shape[0] // 2
    to_x, to_z = pairs(count, lambda i: i ^ 1), pairs(count, lambda i: i ^ 2)
    x_low = lax.ppermute(block[:half], axis, to_x)
    z_high = lax.ppermute(block[half:], axis, to_z)
    x_high = lax.ppermute(block[half:], axis, to_x)
    z_low = lax.ppermute(block[:half], axis, to_z)
    corner = [lax.ppermute(x_low, axis, to_z), lax.ppermute(z_high, axis, to_x)]
    return [block, [x_low, x_high], [z_low, z_high], corner]


def ring_gather(block, axis):
    count, half = lax.axis_size(axis), block.shape[0] // 2
    up = pairs(count, lambda i: (i + 1) % count)
    down = pairs(count, lambda i: (i - 1) % count)
    left_low = lax.ppermute(block[:half], axis, up)
    right_high = lax.ppermute(block[half:], axis, down)
    left_high = lax.ppermute(block[half:], axis, up)
    right_low = lax.ppermute(block[:half], axis, down)
    far = [lax.ppermute(left_low, axis, up), lax.ppermute(right_high, axis, down)]
    return [block, [left_low, left_high], far, [right_low, right_high]]


def joined(block):
    return jnp.concatenate(block, 0) if isinstance(block, list) else block


def two_bit_xor(a, b):
    both = (a % 2) * (b % 2) + 2 * ((a // 2) * (b // 2))
    return a + b - 2 * both


def owners_kernel(side, tiles, part_ref, out_ref, slots, send_sems, recv_sems):
    me_r, me_c, me_t = lax.axis_index("r"), lax.axis_index("c"), lax.axis_index("mesh")
    halves = tiles // 2
    parity = me_t % 2
    incoming = (me_t // side) % 2

    def same(a, b):
        gap = a - b
        return 1 - (gap * gap + 15) // 16

    alone = same(me_t % side, me_c) * same(parity, incoming)
    barrier = pltpu.get_barrier_semaphore()
    for i in range(halves):
        j = 2 * i + parity

        @pl.when(jnp.logical_not(jnp.logical_and(j // side == me_c, me_c + side * (j % side) == me_t)))
        def _():
            pl.semaphore_signal(
                barrier, 1, device_id=(me_r, j // side, me_c + side * (j % side)),
                device_id_type=pl.DeviceIdType.MESH,
            )

    for source in range(halves):

        @pl.when(jnp.logical_not(jnp.logical_and(alone == 1, me_t // 2 == source)))
        def _():
            pl.semaphore_signal(
                barrier, 1, device_id=(me_r, me_t % side, 2 * source + incoming),
                device_id_type=pl.DeviceIdType.MESH,
            )

    pl.semaphore_wait(barrier, 2 * (halves - alone))
    sends = []
    for i in range(halves):
        j = 2 * i + parity
        dest_c = j // side
        dest_t = me_c + side * (j % side)
        to_self = jnp.logical_and(dest_c == me_c, dest_t == me_t)
        copy = pltpu.make_async_remote_copy(
            src_ref=part_ref.at[i],
            dst_ref=slots.at[me_t // 2],
            send_sem=send_sems.at[i],
            recv_sem=recv_sems.at[me_t // 2],
            device_id=(me_r, dest_c, dest_t),
            device_id_type=pl.DeviceIdType.MESH,
        )
        sends.append((copy, to_self, i))

        @pl.when(jnp.logical_not(to_self))
        def _():
            copy.start()

    for copy, to_self, i in sends:

        @pl.when(to_self)
        def _():
            slots[me_t // 2] = part_ref[i]

    mine = alone == 1
    for source in range(halves):
        arrival = pltpu.make_async_remote_copy(
            src_ref=slots.at[source],
            dst_ref=slots.at[source],
            send_sem=send_sems.at[source],
            recv_sem=recv_sems.at[source],
            device_id=(me_r, me_c, me_t),
            device_id_type=pl.DeviceIdType.MESH,
        )

        @pl.when(jnp.logical_not(jnp.logical_and(mine, me_t // 2 == source)))
        def _():
            arrival.wait_recv()

    for copy, to_self, _ in sends:

        @pl.when(jnp.logical_not(to_self))
        def _():
            copy.wait_send()

    acc = slots[0]
    for source in range(1, halves):
        acc = acc + slots[source]
    out_ref[...] = acc


def scatter_to_owners(blocks, side, tiles, scale):
    width = blocks.shape[-1]
    me_r, me_c, me_t = lax.axis_index("r"), lax.axis_index("c"), lax.axis_index("mesh")
    halves = tiles // 2
    index = jnp.arange(halves, dtype=jnp.int32)

    def pieces(parity):
        j = 2 * index + parity
        return blocks[two_bit_xor(me_c, j // side), (me_r - j % side) % side]

    parity = me_t % 2
    kept = (pieces(parity) + lax.ppermute(pieces(1 - parity), "mesh", pairs(tiles, lambda i: i ^ 1))) / scale
    return pl.pallas_call(
        functools.partial(owners_kernel, side, tiles),
        out_shape=jax.ShapeDtypeStruct((width, width), jnp.float32),
        in_specs=[pl.BlockSpec(memory_space=pltpu.VMEM)],
        out_specs=pl.BlockSpec(memory_space=pltpu.VMEM),
        scratch_shapes=[
            pltpu.VMEM((halves, width, width), jnp.float32),
            pltpu.SemaphoreType.DMA((halves,)),
            pltpu.SemaphoreType.DMA((halves,)),
        ],
        compiler_params=pltpu.CompilerParams(collective_id=0, has_side_effects=True),
    )(kept)


def local(snapshots, region_ids, conductivity):
    strip, width = region_ids.shape
    node_rows, group_cols = snapshots.shape
    side = lax.axis_size("c")
    tiles = lax.axis_size("mesh")
    field = snapshots.reshape(strip, width, group_cols)
    weight = weights_of(region_ids, conductivity)
    below = passed_along(field[0], "mesh", -1)
    above = passed_along(field[strip - 1], "mesh", 1)
    weight_above = passed_along(weight[strip - 1], "mesh", 1)
    total = element_terms(
        jnp.concatenate([above[None], field], 0),
        below,
        jnp.concatenate([weight_above[None], weight], 0),
    )
    panel = total[1 : strip + 1, :width].reshape(node_rows, group_cols)
    rows = square_gather(panel, "c")
    cols = ring_gather(snapshots, "r")
    relayed_row, relayed_col = len(rows) - 1, len(cols) // 2

    def product(k1, k2):
        if k1 == relayed_row or k2 == relayed_col:
            half = node_rows // 2
            a, b = rows[k1], cols[k2]
            a = a if isinstance(a, list) else [a[:half], a[half:]]
            b = b if isinstance(b, list) else [b[:half], b[half:]]
            return contract(a[0], b[0]) + contract(a[1], b[1])
        return contract(joined(rows[k1]), joined(cols[k2]))

    blocks = jnp.stack(
        [jnp.stack([product(k1, k2) for k2 in range(side)], 0) for k1 in range(side)], 0
    )
    return scatter_to_owners(blocks, side, tiles, math.sqrt(node_rows * tiles))


def solution(mesh):
    snap = mesh.shape["snap"]
    side = math.isqrt(snap)
    grid = Mesh(
        mesh.devices.reshape(snap // side, side, mesh.shape["mesh"]), ("r", "c", "mesh")
    )
    return jax.shard_map(
        local,
        mesh=grid,
        in_specs=(P("mesh", ("r", "c")), P("mesh", None), P()),
        out_specs=P(("r", "c"), "mesh"),
        check_vma=False,
    )
```

```python
import functools
import math

import jax
import jax.numpy as jnp
from jax import lax
from jax.experimental import pallas as pl
from jax.experimental.pallas import tpu as pltpu
from jax.sharding import Mesh
from jax.sharding import PartitionSpec as P


def passed_along(value, axis, steps):
    count = lax.axis_size(axis)
    first, last = (max(0, -steps), min(count, count - steps))
    return lax.ppermute(value, axis, [(source, source + steps) for source in range(first, last)])


def weights_of(region_ids, conductivity):
    table = jnp.arange(conductivity.shape[0], dtype=jnp.int32)
    picked = jnp.where(
        region_ids[:, :, None] == table[None, None, :],
        conductivity[None, None, :],
        jnp.zeros((), conductivity.dtype),
    )
    return jnp.sum(picked, axis=-1) / 36.0


def element_terms(field, below, weight):
    lower = jnp.concatenate([field, below[None]], 0)
    padded = jnp.pad(lower, ((0, 0), (0, 1), (0, 0)))
    corner_a = padded[:-1, :-1]
    corner_b = padded[:-1, 1:]
    corner_e = padded[1:, :-1]
    corner_d = padded[1:, 1:]
    scaled = weight[:, :, None]
    to_a = scaled * (4.0 * corner_a + 2.0 * corner_b + 2.0 * corner_e + corner_d)
    to_b = scaled * (2.0 * corner_a + 4.0 * corner_b + corner_e + 2.0 * corner_d)
    to_e = scaled * (2.0 * corner_a + corner_b + 4.0 * corner_e + 2.0 * corner_d)
    to_d = scaled * (corner_a + 2.0 * corner_b + 2.0 * corner_e + 4.0 * corner_d)
    total = jnp.pad(to_a, ((0, 1), (0, 1), (0, 0))) + jnp.pad(to_b, ((0, 1), (1, 0), (0, 0)))
    total = (
        total + jnp.pad(to_e, ((1, 0), (0, 1), (0, 0))) + jnp.pad(to_d, ((1, 0), (1, 0), (0, 0)))
    )
    return total


def contract(left, right):
    return lax.dot_general(
        left,
        right,
        (((0,), (0,)), ((), ())),
        precision=lax.Precision.HIGH,
        preferred_element_type=jnp.float32,
    )


def pairs(count, to):
    return [(i, to(i)) for i in range(count)]


def square_gather(block, axis):
    count, half = lax.axis_size(axis), block.shape[0] // 2
    to_x, to_z = pairs(count, lambda i: i ^ 1), pairs(count, lambda i: i ^ 2)
    x_low = lax.ppermute(block[:half], axis, to_x)
    z_high = lax.ppermute(block[half:], axis, to_z)
    x_high = lax.ppermute(block[half:], axis, to_x)
    z_low = lax.ppermute(block[:half], axis, to_z)
    corner = [lax.ppermute(x_low, axis, to_z), lax.ppermute(z_high, axis, to_x)]
    return [block, [x_low, x_high], [z_low, z_high], corner]


def ring_gather(block, axis):
    count, half = lax.axis_size(axis), block.shape[0] // 2
    up = pairs(count, lambda i: (i + 1) % count)
    down = pairs(count, lambda i: (i - 1) % count)
    left_low = lax.ppermute(block[:half], axis, up)
    right_high = lax.ppermute(block[half:], axis, down)
    left_high = lax.ppermute(block[half:], axis, up)
    right_low = lax.ppermute(block[:half], axis, down)
    far = [lax.ppermute(left_low, axis, up), lax.ppermute(right_high, axis, down)]
    return [block, [left_low, left_high], far, [right_low, right_high]]


def joined(block):
    return jnp.concatenate(block, 0) if isinstance(block, list) else block


def two_bit_xor(a, b):
    both = (a % 2) * (b % 2) + 2 * ((a // 2) * (b // 2))
    return a + b - 2 * both


def owners_kernel(side, tiles, part_ref, out_ref, slots, send_sems, recv_sems):
    me_r, me_c, me_t = lax.axis_index("r"), lax.axis_index("c"), lax.axis_index("mesh")
    halves = tiles // 2
    parity = me_t % 2
    incoming = (me_t // side) % 2

    def same(a, b):
        gap = a - b
        return 1 - (gap * gap + 15) // 16

    alone = same(me_t % side, me_c) * same(parity, incoming)
    barrier = pltpu.get_barrier_semaphore()
    for i in range(halves):
        j = 2 * i + parity

        @pl.when(jnp.logical_not(jnp.logical_and(j // side == me_c, me_c + side * (j % side) == me_t)))
        def _():
            pl.semaphore_signal(
                barrier, 1, device_id=(me_r, j // side, me_c + side * (j % side)),
                device_id_type=pl.DeviceIdType.MESH,
            )

    for source in range(halves):

        @pl.when(jnp.logical_not(jnp.logical_and(alone == 1, me_t // 2 == source)))
        def _():
            pl.semaphore_signal(
                barrier, 1, device_id=(me_r, me_t % side, 2 * source + incoming),
                device_id_type=pl.DeviceIdType.MESH,
            )

    pl.semaphore_wait(barrier, 2 * (halves - alone))
    sends = []
    for i in range(halves):
        j = 2 * i + parity
        dest_c = j // side
        dest_t = me_c + side * (j % side)
        to_self = jnp.logical_and(dest_c == me_c, dest_t == me_t)
        copy = pltpu.make_async_remote_copy(
            src_ref=part_ref.at[i],
            dst_ref=slots.at[me_t // 2],
            send_sem=send_sems.at[i],
            recv_sem=recv_sems.at[me_t // 2],
            device_id=(me_r, dest_c, dest_t),
            device_id_type=pl.DeviceIdType.MESH,
        )
        sends.append((copy, to_self, i))

        @pl.when(jnp.logical_not(to_self))
        def _():
            copy.start()

    for copy, to_self, i in sends:

        @pl.when(to_self)
        def _():
            slots[me_t // 2] = part_ref[i]

    mine = alone == 1
    for source in range(halves):
        arrival = pltpu.make_async_remote_copy(
            src_ref=slots.at[source],
            dst_ref=slots.at[source],
            send_sem=send_sems.at[source],
            recv_sem=recv_sems.at[source],
            device_id=(me_r, me_c, me_t),
            device_id_type=pl.DeviceIdType.MESH,
        )

        @pl.when(jnp.logical_not(jnp.logical_and(mine, me_t // 2 == source)))
        def _():
            arrival.wait_recv()

    for copy, to_self, _ in sends:

        @pl.when(jnp.logical_not(to_self))
        def _():
            copy.wait_send()

    acc = slots[0]
    for source in range(1, halves):
        acc = acc + slots[source]
    out_ref[...] = acc


def scatter_to_owners(blocks, side, tiles, scale):
    width = blocks.shape[-1]
    me_r, me_c, me_t = lax.axis_index("r"), lax.axis_index("c"), lax.axis_index("mesh")
    halves = tiles // 2
    index = jnp.arange(halves, dtype=jnp.int32)

    def pieces(parity):
        j = 2 * index + parity
        return blocks[two_bit_xor(me_c, j // side), (me_r - j % side) % side]

    parity = me_t % 2
    kept = (pieces(parity) + lax.ppermute(pieces(1 - parity), "mesh", pairs(tiles, lambda i: i ^ 1))) / scale
    return pl.pallas_call(
        functools.partial(owners_kernel, side, tiles),
        out_shape=jax.ShapeDtypeStruct((width, width), jnp.float32),
        in_specs=[pl.BlockSpec(memory_space=pltpu.VMEM)],
        out_specs=pl.BlockSpec(memory_space=pltpu.VMEM),
        scratch_shapes=[
            pltpu.VMEM((halves, width, width), jnp.float32),
            pltpu.SemaphoreType.DMA((halves,)),
            pltpu.SemaphoreType.DMA((halves,)),
        ],
        compiler_params=pltpu.CompilerParams(collective_id=0, has_side_effects=True),
    )(kept)


def local(snapshots, region_ids, conductivity):
    strip, width = region_ids.shape
    node_rows, group_cols = snapshots.shape
    side = lax.axis_size("c")
    tiles = lax.axis_size("mesh")
    field = snapshots.reshape(strip, width, group_cols)
    weight = weights_of(region_ids, conductivity)
    below = passed_along(field[0], "mesh", -1)
    above = passed_along(field[strip - 1], "mesh", 1)
    region_above = passed_along(region_ids[strip - 1], "mesh", 1)
    has_above = lax.axis_index("mesh") > 0
    weight_above = jnp.where(has_above, weights_of(region_above[None], conductivity)[0], 0.0)
    total = element_terms(
        jnp.concatenate([above[None], field], 0),
        below,
        jnp.concatenate([weight_above[None], weight], 0),
    )
    panel = total[1 : strip + 1, :width].reshape(node_rows, group_cols)
    rows = square_gather(panel, "c")
    cols = ring_gather(snapshots, "r")
    relayed_row, relayed_col = len(rows) - 1, len(cols) // 2

    def product(k1, k2):
        if k1 == relayed_row or k2 == relayed_col:
            half = node_rows // 2
            a, b = rows[k1], cols[k2]
            a = a if isinstance(a, list) else [a[:half], a[half:]]
            b = b if isinstance(b, list) else [b[:half], b[half:]]
            return contract(a[0], b[0]) + contract(a[1], b[1])
        return contract(joined(rows[k1]), joined(cols[k2]))

    blocks = jnp.stack(
        [jnp.stack([product(k1, k2) for k2 in range(side)], 0) for k1 in range(side)], 0
    )
    return scatter_to_owners(blocks, side, tiles, math.sqrt(node_rows * tiles))


def solution(mesh):
    snap = mesh.shape["snap"]
    side = math.isqrt(snap)
    grid = Mesh(
        mesh.devices.reshape(snap // side, side, mesh.shape["mesh"]), ("r", "c", "mesh")
    )
    return jax.shard_map(
        local,
        mesh=grid,
        in_specs=(P("mesh", ("r", "c")), P("mesh", None), P()),
        out_specs=P(("r", "c"), "mesh"),
        check_vma=False,
    )
```
